256 devices in a mesh: dp: 2 (over core), tile: 32 (over x, z), chan: 4 (over y).
Axes of the slice: x: 4, y: 4, z: 8, core: 2. Of those that a mesh axis runs over, the one named last changes fastest.
Arguments:
- pixels: float32 [48, 65536], P(None, ('dp', 'tile')), may hold values from -6 to 6
- tile_slide: int32 [1024], P(('dp', 'tile')), may hold values from 0 to 63, as said below
- tile_count: int32 [64], P(('dp', 'tile')), may hold values from 8 to 16, as said below
- w_patch: float32 [96, 48], P('chan'), may hold values from -0.875 to 0.875
- b_patch: float32 [96], P('chan'), may hold values from -3 to 3
- dw_kernel: float32 [96, 49], P('chan'), may hold values from -0.875 to 0.875
- dw_bias: float32 [96], P('chan'), may hold values from -3 to 3
- layernorm_gain: float32 [96], P('chan'), may hold values from 0.25 to 1.75
- layernorm_bias: float32 [96], P('chan'), may hold values from -3 to 3
- w_up: float32 [384, 96], P('chan'), may hold values from -0.625 to 0.625
- b_up: float32 [384], P('chan'), may hold values from -3 to 3
- w_down: float32 [384, 96], P('chan'), may hold values from -0.3125 to 0.3125
- b_down: float32 [96], P('chan'), may hold values from -3 to 3
- w_head: float32 [96], P('chan'), may hold values from -3 to 3
- target: float32 [128], P(('dp', 'tile')), may hold values from -4 to 4
Outputs:
- g_w_patch: float32 [96, 48], P('chan')
- g_b_patch: float32 [96], P('chan')
- g_dw_kernel: float32 [96, 49], P('chan')
- g_dw_bias: float32 [96], P('chan')
- g_ln_gain: float32 [96], P('chan')
- g_ln_bias: float32 [96], P('chan')
- g_w_up: float32 [384, 96], P('chan')
- g_b_up: float32 [384], P('chan')
- g_w_down: float32 [384, 96], P('chan')
- g_b_down: float32 [96], P('chan')
- g_w_head: float32 [96], P('chan')
- loss: float32 [], replicated
The draws below stay inside these ranges and needn't reach their ends.
Inputs may be any that keep to these rules, and one draw needn't show every extreme that they name: `tile_slide`: in every slide group a run of 4 consecutive slides, neither the group's first nor its last, receives no slot; other slides may receive none too. `tile_count`: at least 8 live slots a device; some device has all 16 live in every draw.
All inputs are finite; a program needn't handle non-finite values.
Results may differ from the reference program's by a relative error of at most 0.00029.
Values sent between devices are 32-bit elements; how exact they have to be, the bound alone decides.
A program may use at most 64 MiB of HBM per device.

```python
import jax
import jax.numpy as jnp
from jax import lax

C = 96
HID = 384
PATCH_IN = 48
SIDE = 8
TILE_DEV = 16
TILES = 1024
SG = 64
SLIDES = 128
N_TILE = 32


def draw_tile_count(key, part):
    devices = TILES // TILE_DEV
    counts = jax.random.randint(key, (devices,), TILE_DEV // 2, TILE_DEV + 1)
    fullest = jax.random.randint(jax.random.fold_in(key, 7), (), 0, devices)
    return jnp.where(jnp.arange(devices) == fullest, TILE_DEV, counts).astype(jnp.int32)


def draw_tile_slide(key, part):
    groups = SLIDES // SG
    per_group = TILES // groups
    empty_run = max(1, SG // 16)
    raw_slide = jax.random.randint(key, (groups, per_group), 0, SG - empty_run)
    run_start = jax.random.randint(jax.random.fold_in(key, 11), (groups, 1), 1, SG - empty_run)
    slide_ids = jnp.where(raw_slide < run_start, raw_slide, raw_slide + empty_run).reshape(TILES)
    slide_ids = slide_ids.at[0].set(0).at[TILES - 1].set(SG - 1)
    return slide_ids.astype(jnp.int32)


def steps_of(rng, extent, split, low, top_value):
    loudness, own = 1.0, jax.random.fold_in(rng, 6)
    for dim, blocks in split:
        heights = jnp.exp(jax.random.uniform(jax.random.fold_in(own, dim), (blocks,), jnp.float32, low / len(split), top_value / len(split)))
        loudness = loudness * jnp.repeat(heights, extent[dim] // blocks).reshape([-1 if axis == dim else 1 for axis in range(len(extent))])
    return loudness


def noise(rng, extent, width, reach, pieces=(), kind=jnp.bfloat16):
    entries = jax.random.normal(rng, extent, jnp.float32) * width
    if len(pieces) > 0:
        entries = steps_of(rng, extent, pieces, -0.22, 0.18) * entries
    return jnp.clip(entries, min=-reach, max=reach).astype(kind)


def setup_inputs(seed: int = 0) -> dict:
    seeds = jax.random.split(jax.random.key(seed), 16)
    pixels = noise(seeds[0], (PATCH_IN, TILES * SIDE * SIDE), 1.0, 6.0, ((1, 64),), jnp.float32)
    tile_slide = draw_tile_slide(jax.random.fold_in(seeds[15], 71), 0)
    tile_count = draw_tile_count(jax.random.fold_in(seeds[15], 71), 0)
    w_patch = noise(seeds[3], (C, PATCH_IN), PATCH_IN ** -0.5, 0.875, ((0, 4),), jnp.float32)
    b_patch = noise(seeds[4], (C,), 0.5, 3.0, ((0, 4),), jnp.float32)
    dw_kernel = noise(seeds[5], (C, 49), 49 ** -0.5, 0.875, ((0, 4),), jnp.float32)
    dw_bias = noise(seeds[6], (C,), 0.5, 3.0, ((0, 4),), jnp.float32)
    layernorm_gain = jnp.clip(1.0 + 0.15 * jax.random.normal(seeds[7], (C,), jnp.float32), 0.25, 1.75)
    layernorm_bias = noise(seeds[8], (C,), 0.5, 3.0, ((0, 4),), jnp.float32)
    w_up = noise(seeds[9], (HID, C), C ** -0.5, 0.625, ((0, 4),), jnp.float32)
    b_up = noise(seeds[10], (HID,), 0.5, 3.0, ((0, 4),), jnp.float32)
    w_down = noise(seeds[11], (HID, C), HID ** -0.5, 0.3125, ((0, 4),), jnp.float32)
    b_down = noise(seeds[12], (C,), 0.5, 3.0, ((0, 4),), jnp.float32)
    w_head = noise(seeds[13], (C,), 0.5, 3.0, ((0, 4),), jnp.float32)
    target = noise(seeds[14], (SLIDES,), 1.0, 4.0, ((0, 64),), jnp.float32)
    return dict(pixels=pixels, tile_slide=tile_slide, tile_count=tile_count, w_patch=w_patch, b_patch=b_patch, dw_kernel=dw_kernel, dw_bias=dw_bias, layernorm_gain=layernorm_gain, layernorm_bias=layernorm_bias, w_up=w_up, b_up=b_up, w_down=w_down, b_down=b_down, w_head=w_head, target=target)


epsilon = 1e-06
highest = lax.Precision.HIGHEST

def depthwise(stem_grid, kernel, bias):
    side_len = stem_grid.shape[-1]
    padded = jnp.pad(stem_grid, ((0, 0), (0, 0), (3, 3), (3, 3)))
    total = jnp.zeros_like(stem_grid)
    for kernel_row in range(7):
        for kernel_col in range(7):
            weight_tap = kernel[:, kernel_row * 7 + kernel_col][:, None, None, None]
            total = total + weight_tap * padded[:, :, kernel_row:kernel_row + side_len, kernel_col:kernel_col + side_len]
    return total + bias[:, None, None, None]

def block_pooled(params, block_pixels):
    w_patch, b_patch, dw_kernel, dw_bias, layernorm_gain, layernorm_bias, w_up, b_up, w_down, b_down = params
    channel_width = w_patch.shape[0]
    tile_num = block_pixels.shape[1] // (SIDE * SIDE)
    stem = jnp.dot(w_patch, block_pixels, precision=highest) + b_patch[:, None]
    mixed_features = depthwise(stem.reshape(channel_width, tile_num, SIDE, SIDE), dw_kernel, dw_bias).reshape(channel_width, -1)
    average_value = lax.optimization_barrier(jnp.mean(mixed_features, axis=0))
    variance = lax.optimization_barrier(jnp.mean(mixed_features * mixed_features, axis=0)) - average_value * average_value
    normalized_rows = (mixed_features - average_value) * lax.rsqrt(variance + epsilon) * layernorm_gain[:, None] + layernorm_bias[:, None]
    pre_act = jnp.dot(w_up, normalized_rows, precision=highest) + b_up[:, None]
    hidden = jax.nn.gelu(pre_act, approximate=False)
    features = stem + jnp.dot(w_down.T, hidden, precision=highest) + b_down[:, None]
    return lax.optimization_barrier(jnp.mean(features.reshape(channel_width, tile_num, SIDE * SIDE), axis=2))

def reference(pixels, tile_slide, tile_count, w_patch, b_patch, dw_kernel, dw_bias, layernorm_gain, layernorm_bias, w_up, b_up, w_down, b_down, w_head, target):
    params = (w_patch, b_patch, dw_kernel, dw_bias, layernorm_gain, layernorm_bias, w_up, b_up, w_down, b_down)
    blocks = TILES // TILE_DEV
    pix_blocks = pixels.reshape(PATCH_IN, blocks, TILE_DEV * SIDE * SIDE).transpose(1, 0, 2)
    pooled = lax.map(lambda block_pixels: block_pooled(params, block_pixels), pix_blocks)
    live = (jnp.arange(TILE_DEV, dtype=jnp.int32)[None, :] < tile_count[:, None]).astype(jnp.float32)
    group = jnp.arange(blocks, dtype=jnp.int32) // N_TILE
    slide_ids = group[:, None] * SG + tile_slide.reshape(blocks, TILE_DEV)
    onehot = (slide_ids[:, :, None] == jnp.arange(SLIDES, dtype=jnp.int32)[None, None, :]).astype(jnp.float32) * live[:, :, None]
    sums = jnp.einsum('bct,bts->sc', pooled, onehot, precision=highest)
    counts = jnp.maximum(lax.optimization_barrier(jnp.sum(onehot, axis=(0, 1))), 1.0)
    slide_feat = sums / counts[:, None]
    logit = jnp.dot(slide_feat, w_head, precision=highest)
    error = logit - target
    loss = 0.5 * jnp.sum(error * error) / SLIDES
    d_logit = error / SLIDES
    g_w_head = jnp.dot(slide_feat.T, d_logit, precision=highest)
    d_sums = d_logit[:, None] * w_head[None, :] / counts[:, None]
    d_pooled = jnp.einsum('bts,sc->bct', onehot, d_sums, precision=highest)

    def backward(carry, inputs):
        block_pixels, block_grad = inputs
        unused, pull = jax.vjp(lambda weights: block_pooled(weights, block_pixels), params)
        grads = pull(block_grad)[0]
        return (jax.tree.map(jnp.add, carry, grads), None)
    zeros = jax.tree.map(jnp.zeros_like, params)
    grads, unused = lax.scan(backward, zeros, (pix_blocks, d_pooled))
    return (grads[0], grads[1], grads[2], grads[3], grads[4], grads[5], grads[6], grads[7], grads[8], grads[9], g_w_head, loss)
```

```python
import jax
import jax.numpy as jnp
import numpy as np
from jax import lax
from jax.sharding import Mesh
from jax.sharding import PartitionSpec as P

SIDE = 8
X_SPAN = 4


epsilon = 1e-06
highest = lax.Precision.HIGHEST


def depthwise(stem_grid, kernel, bias):
    side_len = stem_grid.shape[-1]
    padded = jnp.pad(stem_grid, ((0, 0), (0, 0), (3, 3), (3, 3)))
    total = jnp.zeros_like(stem_grid)
    for kernel_row in range(7):
        for kernel_col in range(7):
            weight_tap = kernel[:, kernel_row * 7 + kernel_col][:, None, None, None]
            total = (
                total
                + weight_tap
                * padded[
                    :, :, kernel_row : kernel_row + side_len, kernel_col : kernel_col + side_len
                ]
            )
    return total + bias[:, None, None, None]


def block_pooled(params, pixels):
    w_patch, b_patch, dw_kernel, dw_bias, gain, shift, w_up, b_up, w_down, b_down = params
    width = w_patch.shape[0]
    tile_num = pixels.shape[1] // (SIDE * SIDE)
    stem = jnp.dot(w_patch, pixels, precision=highest) + b_patch[:, None]
    mixed = depthwise(stem.reshape(width, tile_num, SIDE, SIDE), dw_kernel, dw_bias).reshape(
        width, -1
    )
    average_value = jnp.mean(mixed, axis=0)
    variance = jnp.mean(mixed * mixed, axis=0) - average_value * average_value
    normed = (mixed - average_value) * lax.rsqrt(variance + epsilon) * gain[:, None] + shift[
        :, None
    ]
    pre_act = jnp.dot(w_up, normed, precision=highest) + b_up[:, None]
    hidden = jax.nn.gelu(pre_act, approximate=False)
    features = stem + jnp.dot(w_down.T, hidden, precision=highest) + b_down[:, None]
    return jnp.mean(features.reshape(width, tile_num, SIDE * SIDE), axis=2)


def psum_steps(value, axes):
    for axis in axes:
        value = lax.psum(value, axis)
    return value


def per_device(
    pixels,
    tile_slide,
    tile_count,
    w_patch,
    b_patch,
    dw_kernel,
    dw_bias,
    layernorm_gain,
    layernorm_bias,
    w_up,
    b_up,
    w_down,
    b_down,
    w_head,
    target,
):
    chan_count = lax.axis_size("chan")
    chan = lax.axis_index("chan")
    tile = lax.axis_index("tx") * lax.axis_size("tz") + lax.axis_index("tz")
    slot_count = tile_slide.shape[0]
    slots = slot_count // chan_count
    area = SIDE * SIDE
    slide_dev = target.shape[0]
    group_slides = slide_dev * lax.axis_size("tx") * lax.axis_size("tz")
    all_slides = group_slides * lax.axis_size("dp")

    shards = (
        w_patch,
        b_patch,
        dw_kernel,
        dw_bias,
        layernorm_gain,
        layernorm_bias,
        w_up,
        b_up,
        w_down,
        b_down,
        w_head,
    )
    sizes = [s.size for s in shards]
    packed = jnp.concatenate([s.reshape(1, -1) for s in shards], axis=1)
    gathered = lax.all_gather(packed, "chan", axis=0, tiled=True)
    full = []
    offset = 0
    for s, n in zip(shards, sizes):
        full.append(gathered[:, offset : offset + n].reshape((chan_count * s.shape[0],) + s.shape[1:]))
        offset += n
    params = tuple(full[:10])
    head = full[10]

    my_pixels = lax.dynamic_slice_in_dim(pixels, chan * slots * area, slots * area, axis=1)
    my_slide = lax.dynamic_slice_in_dim(tile_slide, chan * slots, slots)
    slot_index = chan * slots + jnp.arange(slots, dtype=jnp.int32)
    live = (slot_index < tile_count[0]).astype(jnp.float32)
    onehot = (my_slide[:, None] == jnp.arange(group_slides, dtype=jnp.int32)[None, :]).astype(
        jnp.float32
    ) * live[:, None]

    pooled, pull = jax.vjp(lambda p: block_pooled(p, my_pixels), params)
    slide_part = jnp.dot(onehot.T, pooled.T, precision=highest)
    placed = lax.dynamic_update_slice_in_dim(
        jnp.zeros((group_slides,), jnp.float32),
        jnp.where(chan == 0, target, 0.0),
        tile * slide_dev,
        axis=0,
    )
    slide_pack = jnp.concatenate(
        [slide_part, jnp.sum(onehot, axis=0)[:, None], placed[:, None]], axis=1
    )
    slide_pack = psum_steps(slide_pack, ("chan", "tx", "tz"))
    width = slide_part.shape[1]
    sums = slide_pack[:, :width]
    counts = jnp.maximum(slide_pack[:, width], 1.0)
    target_all = slide_pack[:, width + 1]

    slide_feat = sums / counts[:, None]
    logit = jnp.dot(slide_feat, head, precision=highest)
    error = logit - target_all
    loss_part = 0.5 * jnp.sum(error * error) / all_slides
    d_logit = error / all_slides
    g_head = jnp.dot(slide_feat.T, d_logit, precision=highest)
    d_sums = d_logit[:, None] * head[None, :] / counts[:, None]
    d_pooled = jnp.dot(onehot, d_sums, precision=highest).T
    grads = pull(d_pooled)[0]

    lead = tile == 0
    g_head = jnp.where(lead & (chan == 0), g_head, 0.0)
    flat = jnp.concatenate(
        [g.reshape(chan_count, -1) for g in grads] + [g_head.reshape(chan_count, -1)], axis=1
    )
    mine = lax.psum_scatter(flat, "chan", scatter_dimension=0, tiled=True).reshape(-1)
    mine = jnp.concatenate([mine, jnp.where(lead, loss_part, 0.0)[None]])
    mine = psum_steps(mine, ("dp", "tx", "tz"))

    outs = []
    offset = 0
    for s in shards[:10] + shards[10:]:
        n = s.size
        outs.append(mine[offset : offset + n].reshape(s.shape))
        offset += n
    outs.append(mine[offset])
    return tuple(outs)


def solution(mesh):
    devices = np.asarray(mesh.devices)
    dp, tiles, chan = devices.shape
    grid = Mesh(devices.reshape(dp, X_SPAN, tiles // X_SPAN, chan), ("dp", "tx", "tz", "chan"))
    rows = ("dp", "tx", "tz")
    in_specs = (
        P(None, rows),
        P(rows),
        P(rows),
        P("chan", None),
        P("chan"),
        P("chan", None),
        P("chan"),
        P("chan"),
        P("chan"),
        P("chan", None),
        P("chan"),
        P("chan", None),
        P("chan"),
        P("chan"),
        P(rows),
    )
    out_specs = (
        P("chan", None),
        P("chan"),
        P("chan", None),
        P("chan"),
        P("chan"),
        P("chan"),
        P("chan", None),
        P("chan"),
        P("chan", None),
        P("chan"),
        P("chan"),
        P(),
    )
    return jax.shard_map(
        per_device, mesh=grid, in_specs=in_specs, out_specs=out_specs, check_vma=False
    )
```

```python
import jax
import jax.numpy as jnp
import numpy as np
from jax import lax
from jax.sharding import Mesh
from jax.sharding import PartitionSpec as P

SIDE = 8
X_SPAN = 4


epsilon = 1e-06
highest = lax.Precision.HIGHEST


def depthwise(stem_grid, kernel, bias):
    side_len = stem_grid.shape[-1]
    padded = jnp.pad(stem_grid, ((0, 0), (0, 0), (3, 3), (3, 3)))
    total = jnp.zeros_like(stem_grid)
    for kernel_row in range(7):
        for kernel_col in range(7):
            weight_tap = kernel[:, kernel_row * 7 + kernel_col][:, None, None, None]
            total = (
                total
                + weight_tap
                * padded[
                    :, :, kernel_row : kernel_row + side_len, kernel_col : kernel_col + side_len
                ]
            )
    return total + bias[:, None, None, None]


def block_pooled(params, pixels):
    w_patch, b_patch, dw_kernel, dw_bias, gain, shift, w_up, b_up, w_down, b_down = params
    width = w_patch.shape[0]
    tile_num = pixels.shape[1] // (SIDE * SIDE)
    stem = jnp.dot(w_patch, pixels, precision=highest) + b_patch[:, None]
    mixed = depthwise(stem.reshape(width, tile_num, SIDE, SIDE), dw_kernel, dw_bias).reshape(
        width, -1
    )
    average_value = jnp.mean(mixed, axis=0)
    variance = jnp.mean(mixed * mixed, axis=0) - average_value * average_value
    normed = (mixed - average_value) * lax.rsqrt(variance + epsilon) * gain[:, None] + shift[
        :, None
    ]
    pre_act = jnp.dot(w_up, normed, precision=highest) + b_up[:, None]
    hidden = jax.nn.gelu(pre_act, approximate=False)
    features = stem + jnp.dot(w_down.T, hidden, precision=highest) + b_down[:, None]
    return jnp.mean(features.reshape(width, tile_num, SIDE * SIDE), axis=2)


def spread_sum(value, axis):
    count = lax.axis_size(axis)
    copies = jnp.broadcast_to(value[None], (count,) + value.shape)
    return jnp.sum(lax.all_to_all(copies, axis, 0, 0, tiled=True), axis=0)


def psum_steps(value, axes):
    for axis in axes:
        value = spread_sum(value, axis)
    return value


def scatter_sum(value, axis):
    return jnp.sum(lax.all_to_all(value, axis, 0, 0, tiled=True), axis=0)


def per_device(
    pixels,
    tile_slide,
    tile_count,
    w_patch,
    b_patch,
    dw_kernel,
    dw_bias,
    layernorm_gain,
    layernorm_bias,
    w_up,
    b_up,
    w_down,
    b_down,
    w_head,
    target,
):
    chan_count = lax.axis_size("chan")
    chan = lax.axis_index("chan")
    tile = lax.axis_index("tx") * lax.axis_size("tz") + lax.axis_index("tz")
    slot_count = tile_slide.shape[0]
    slots = slot_count // chan_count
    area = SIDE * SIDE
    slide_dev = target.shape[0]
    group_slides = slide_dev * lax.axis_size("tx") * lax.axis_size("tz")
    all_slides = group_slides * lax.axis_size("dp")

    shards = (
        w_patch,
        b_patch,
        dw_kernel,
        dw_bias,
        layernorm_gain,
        layernorm_bias,
        w_up,
        b_up,
        w_down,
        b_down,
        w_head,
    )
    sizes = [s.size for s in shards]
    packed = jnp.concatenate([s.reshape(1, -1) for s in shards], axis=1)
    gathered = lax.all_gather(packed, "chan", axis=0, tiled=True)
    full = []
    offset = 0
    for s, n in zip(shards, sizes):
        full.append(gathered[:, offset : offset + n].reshape((chan_count * s.shape[0],) + s.shape[1:]))
        offset += n
    params = tuple(full[:10])
    head = full[10]

    my_pixels = lax.dynamic_slice_in_dim(pixels, chan * slots * area, slots * area, axis=1)
    my_slide = lax.dynamic_slice_in_dim(tile_slide, chan * slots, slots)
    slot_index = chan * slots + jnp.arange(slots, dtype=jnp.int32)
    live = (slot_index < tile_count[0]).astype(jnp.float32)
    onehot = (my_slide[:, None] == jnp.arange(group_slides, dtype=jnp.int32)[None, :]).astype(
        jnp.float32
    ) * live[:, None]

    pooled, pull = jax.vjp(lambda p: block_pooled(p, my_pixels), params)
    slide_part = jnp.dot(onehot.T, pooled.T, precision=highest)
    placed = lax.dynamic_update_slice_in_dim(
        jnp.zeros((group_slides,), jnp.float32),
        jnp.where(chan == 0, target, 0.0),
        tile * slide_dev,
        axis=0,
    )
    slide_pack = jnp.concatenate(
        [slide_part, jnp.sum(onehot, axis=0)[:, None], placed[:, None]], axis=1
    )
    slide_pack = psum_steps(slide_pack, ("chan", "tx", "tz"))
    width = slide_part.shape[1]
    sums = slide_pack[:, :width]
    counts = jnp.maximum(slide_pack[:, width], 1.0)
    target_all = slide_pack[:, width + 1]

    slide_feat = sums / counts[:, None]
    logit = jnp.dot(slide_feat, head, precision=highest)
    error = logit - target_all
    loss_part = 0.5 * jnp.sum(error * error) / all_slides
    d_logit = error / all_slides
    g_head = jnp.dot(slide_feat.T, d_logit, precision=highest)
    d_sums = d_logit[:, None] * head[None, :] / counts[:, None]
    d_pooled = jnp.dot(onehot, d_sums, precision=highest).T
    grads = pull(d_pooled)[0]

    lead = tile == 0
    g_head = jnp.where(lead & (chan == 0), g_head, 0.0)
    flat = jnp.concatenate(
        [g.reshape(chan_count, -1) for g in grads] + [g_head.reshape(chan_count, -1)], axis=1
    )
    mine = scatter_sum(flat, "chan")
    mine = jnp.concatenate([mine, jnp.where(lead, loss_part, 0.0)[None]])
    mine = psum_steps(mine, ("dp", "tx", "tz"))

    outs = []
    offset = 0
    for s in shards[:10] + shards[10:]:
        n = s.size
        outs.append(mine[offset : offset + n].reshape(s.shape))
        offset += n
    outs.append(mine[offset])
    return tuple(outs)


def solution(mesh):
    devices = np.asarray(mesh.devices)
    dp, tiles, chan = devices.shape
    grid = Mesh(devices.reshape(dp, X_SPAN, tiles // X_SPAN, chan), ("dp", "tx", "tz", "chan"))
    rows = ("dp", "tx", "tz")
    in_specs = (
        P(None, rows),
        P(rows),
        P(rows),
        P("chan", None),
        P("chan"),
        P("chan", None),
        P("chan"),
        P("chan"),
        P("chan"),
        P("chan", None),
        P("chan"),
        P("chan", None),
        P("chan"),
        P("chan"),
        P(rows),
    )
    out_specs = (
        P("chan", None),
        P("chan"),
        P("chan", None),
        P("chan"),
        P("chan"),
        P("chan"),
        P("chan", None),
        P("chan"),
        P("chan", None),
        P("chan"),
        P("chan"),
        P(),
    )
    return jax.shard_map(
        per_device, mesh=grid, in_specs=in_specs, out_specs=out_specs, check_vma=False
    )
```

```python
import jax
import jax.numpy as jnp
import numpy as np
from jax import lax
from jax.sharding import Mesh
from jax.sharding import PartitionSpec as P

SIDE = 8
X_SPAN = 4


epsilon = 1e-06
highest = lax.Precision.HIGHEST


def depthwise(stem_grid, kernel, bias):
    side_len = stem_grid.shape[-1]
    padded = jnp.pad(stem_grid, ((0, 0), (0, 0), (3, 3), (3, 3)))
    total = jnp.zeros_like(stem_grid)
    for kernel_row in range(7):
        for kernel_col in range(7):
            weight_tap = kernel[:, kernel_row * 7 + kernel_col][:, None, None, None]
            total = (
                total
                + weight_tap
                * padded[
                    :, :, kernel_row : kernel_row + side_len, kernel_col : kernel_col + side_len
                ]
            )
    return total + bias[:, None, None, None]


def block_pooled(params, pixels):
    w_patch, b_patch, dw_kernel, dw_bias, gain, shift, w_up, b_up, w_down, b_down = params
    width = w_patch.shape[0]
    tile_num = pixels.shape[1] // (SIDE * SIDE)
    stem = jnp.dot(w_patch, pixels, precision=highest) + b_patch[:, None]
    mixed = depthwise(stem.reshape(width, tile_num, SIDE, SIDE), dw_kernel, dw_bias).reshape(
        width, -1
    )
    average_value = jnp.mean(mixed, axis=0)
    variance = jnp.mean(mixed * mixed, axis=0) - average_value * average_value
    normed = (mixed - average_value) * lax.rsqrt(variance + epsilon) * gain[:, None] + shift[
        :, None
    ]
    pre_act = jnp.dot(w_up, normed, precision=highest) + b_up[:, None]
    hidden = jax.nn.gelu(pre_act, approximate=False)
    features = stem + jnp.dot(w_down.T, hidden, precision=highest) + b_down[:, None]
    return jnp.mean(features.reshape(width, tile_num, SIDE * SIDE), axis=2)


def spread_sum(value, axis):
    count = lax.psum(1, axis)
    copies = jnp.broadcast_to(value[None], (count,) + value.shape)
    return jnp.sum(lax.all_to_all(copies, axis, 0, 0, tiled=True), axis=0)


def psum_steps(value, axes):
    for axis in axes:
        value = spread_sum(value, axis)
    return value


def scatter_sum(value, axis):
    return jnp.sum(lax.all_to_all(value, axis, 0, 0, tiled=True), axis=0)


def gather_chan(shards, chan_count, spread):
    packed = jnp.concatenate([s.reshape(1, -1) for s in shards], axis=1)
    if spread:
        copies = jnp.broadcast_to(packed, (chan_count, packed.shape[1]))
        gathered = lax.all_to_all(copies, "chan", 0, 0, tiled=True)
    else:
        gathered = lax.all_gather(packed, "chan", axis=0, tiled=True)
    full = []
    offset = 0
    for s in shards:
        n = s.size
        full.append(
            gathered[:, offset : offset + n].reshape((chan_count * s.shape[0],) + s.shape[1:])
        )
        offset += n
    return tuple(full)


def per_device(
    pixels,
    tile_slide,
    tile_count,
    w_patch,
    b_patch,
    dw_kernel,
    dw_bias,
    layernorm_gain,
    layernorm_bias,
    w_up,
    b_up,
    w_down,
    b_down,
    w_head,
    target,
):
    chan_count = lax.axis_size("chan")
    chan = lax.axis_index("chan")
    tile = lax.axis_index("tx") * lax.axis_size("tz") + lax.axis_index("tz")
    slot_count = tile_slide.shape[0]
    slots = slot_count // chan_count
    area = SIDE * SIDE
    slide_dev = target.shape[0]
    group_slides = slide_dev * lax.axis_size("tx") * lax.axis_size("tz")
    all_slides = group_slides * lax.axis_size("dp")

    shards = (
        w_patch,
        b_patch,
        dw_kernel,
        dw_bias,
        layernorm_gain,
        layernorm_bias,
        w_up,
        b_up,
        w_down,
        b_down,
        w_head,
    )
    full = gather_chan(shards[:6], chan_count, spread=False) + gather_chan(
        shards[6:], chan_count, spread=True
    )
    params = tuple(full[:10])
    head = full[10]

    my_pixels = lax.dynamic_slice_in_dim(pixels, chan * slots * area, slots * area, axis=1)
    my_slide = lax.dynamic_slice_in_dim(tile_slide, chan * slots, slots)
    slot_index = chan * slots + jnp.arange(slots, dtype=jnp.int32)
    live = (slot_index < tile_count[0]).astype(jnp.float32)
    onehot = (my_slide[:, None] == jnp.arange(group_slides, dtype=jnp.int32)[None, :]).astype(
        jnp.float32
    ) * live[:, None]

    pooled, pull = jax.vjp(lambda p: block_pooled(p, my_pixels), params)
    slide_part = jnp.dot(onehot.T, pooled.T, precision=highest)
    placed = lax.dynamic_update_slice_in_dim(
        jnp.zeros((group_slides,), jnp.float32),
        jnp.where(chan == 0, target, 0.0),
        tile * slide_dev,
        axis=0,
    )
    slide_pack = jnp.concatenate(
        [slide_part, jnp.sum(onehot, axis=0)[:, None], placed[:, None]], axis=1
    )
    slide_pack = psum_steps(slide_pack, (("chan", "tx"), "tz"))
    width = slide_part.shape[1]
    sums = slide_pack[:, :width]
    counts = jnp.maximum(slide_pack[:, width], 1.0)
    target_all = slide_pack[:, width + 1]

    slide_feat = sums / counts[:, None]
    logit = jnp.dot(slide_feat, head, precision=highest)
    error = logit - target_all
    loss_part = 0.5 * jnp.sum(error * error) / all_slides
    d_logit = error / all_slides
    g_head = jnp.dot(slide_feat.T, d_logit, precision=highest)
    d_sums = d_logit[:, None] * head[None, :] / counts[:, None]
    d_pooled = jnp.dot(onehot, d_sums, precision=highest).T
    grads = pull(d_pooled)[0]

    lead = tile == 0
    g_head = jnp.where(lead & (chan == 0), g_head, 0.0)
    flat = jnp.concatenate(
        [g.reshape(chan_count, -1) for g in grads] + [g_head.reshape(chan_count, -1)], axis=1
    )
    mine = scatter_sum(flat, "chan")
    mine = jnp.concatenate([mine, jnp.where(lead, loss_part, 0.0)[None]])
    mine = psum_steps(mine, ("dp", "tx", "tz"))

    outs = []
    offset = 0
    for s in shards[:10] + shards[10:]:
        n = s.size
        outs.append(mine[offset : offset + n].reshape(s.shape))
        offset += n
    outs.append(mine[offset])
    return tuple(outs)


def solution(mesh):
    devices = np.asarray(mesh.devices)
    dp, tiles, chan = devices.shape
    grid = Mesh(devices.reshape(dp, X_SPAN, tiles // X_SPAN, chan), ("dp", "tx", "tz", "chan"))
    rows = ("dp", "tx", "tz")
    in_specs = (
        P(None, rows),
        P(rows),
        P(rows),
        P("chan", None),
        P("chan"),
        P("chan", None),
        P("chan"),
        P("chan"),
        P("chan"),
        P("chan", None),
        P("chan"),
        P("chan", None),
        P("chan"),
        P("chan"),
        P(rows),
    )
    out_specs = (
        P("chan", None),
        P("chan"),
        P("chan", None),
        P("chan"),
        P("chan"),
        P("chan"),
        P("chan", None),
        P("chan"),
        P("chan", None),
        P("chan"),
        P("chan"),
        P(),
    )
    return jax.shard_map(
        per_device, mesh=grid, in_specs=in_specs, out_specs=out_specs, check_vma=False
    )
```

```python
import jax
import jax.numpy as jnp
import numpy as np
from jax import lax
from jax.sharding import Mesh
from jax.sharding import PartitionSpec as P

SIDE = 8
X_SPAN = 4


epsilon = 1e-06
highest = lax.Precision.HIGHEST


def depthwise(stem_grid, kernel, bias):
    side_len = stem_grid.shape[-1]
    padded = jnp.pad(stem_grid, ((0, 0), (0, 0), (3, 3), (3, 3)))
    total = jnp.zeros_like(stem_grid)
    for kernel_row in range(7):
        for kernel_col in range(7):
            weight_tap = kernel[:, kernel_row * 7 + kernel_col][:, None, None, None]
            total = (
                total
                + weight_tap
                * padded[
                    :, :, kernel_row : kernel_row + side_len, kernel_col : kernel_col + side_len
                ]
            )
    return total + bias[:, None, None, None]


def block_pooled(params, pixels):
    w_patch, b_patch, dw_kernel, dw_bias, gain, shift, w_up, b_up, w_down, b_down = params
    width = w_patch.shape[0]
    tile_num = pixels.shape[1] // (SIDE * SIDE)
    stem = jnp.dot(w_patch, pixels, precision=highest) + b_patch[:, None]
    mixed = depthwise(stem.reshape(width, tile_num, SIDE, SIDE), dw_kernel, dw_bias).reshape(
        width, -1
    )
    average_value = jnp.mean(mixed, axis=0)
    variance = jnp.mean(mixed * mixed, axis=0) - average_value * average_value
    normed = (mixed - average_value) * lax.rsqrt(variance + epsilon) * gain[:, None] + shift[
        :, None
    ]
    pre_act = jnp.dot(w_up, normed, precision=highest) + b_up[:, None]
    hidden = jax.nn.gelu(pre_act, approximate=False)
    features = stem + jnp.dot(w_down.T, hidden, precision=highest) + b_down[:, None]
    return jnp.mean(features.reshape(width, tile_num, SIDE * SIDE), axis=2)


def spread_sum(value, axis):
    count = lax.psum(1, axis)
    copies = jnp.broadcast_to(value[None], (count,) + value.shape)
    return jnp.sum(lax.all_to_all(copies, axis, 0, 0, tiled=True), axis=0)


def psum_steps(value, axes):
    for axis in axes:
        value = spread_sum(value, axis)
    return value


def scatter_sum(value, axis):
    return jnp.sum(lax.all_to_all(value, axis, 0, 0, tiled=True), axis=0)


def gather_chan(shards, chan_count, spread):
    packed = jnp.concatenate([s.reshape(1, -1) for s in shards], axis=1)
    if spread:
        copies = jnp.broadcast_to(packed, (chan_count, packed.shape[1]))
        gathered = lax.all_to_all(copies, "chan", 0, 0, tiled=True)
    else:
        gathered = lax.all_gather(packed, "chan", axis=0, tiled=True)
    full = []
    offset = 0
    for s in shards:
        n = s.size
        full.append(
            gathered[:, offset : offset + n].reshape((chan_count * s.shape[0],) + s.shape[1:])
        )
        offset += n
    return tuple(full)


def per_device(
    pixels,
    tile_slide,
    tile_count,
    w_patch,
    b_patch,
    dw_kernel,
    dw_bias,
    layernorm_gain,
    layernorm_bias,
    w_up,
    b_up,
    w_down,
    b_down,
    w_head,
    target,
):
    chan_count = lax.axis_size("chan")
    chan = lax.axis_index("chan")
    tile = lax.axis_index("tx") * lax.axis_size("tz") + lax.axis_index("tz")
    slot_count = tile_slide.shape[0]
    slots = slot_count // chan_count
    area = SIDE * SIDE
    slide_dev = target.shape[0]
    group_slides = slide_dev * lax.axis_size("tx") * lax.axis_size("tz")
    all_slides = group_slides * lax.axis_size("dp")

    shards = (
        w_patch,
        b_patch,
        dw_kernel,
        dw_bias,
        layernorm_gain,
        layernorm_bias,
        w_up,
        b_up,
        w_down,
        b_down,
        w_head,
    )
    full = gather_chan(shards, chan_count, spread=True)
    params = tuple(full[:10])
    head = full[10]

    my_pixels = lax.dynamic_slice_in_dim(pixels, chan * slots * area, slots * area, axis=1)
    my_slide = lax.dynamic_slice_in_dim(tile_slide, chan * slots, slots)
    slot_index = chan * slots + jnp.arange(slots, dtype=jnp.int32)
    live = (slot_index < tile_count[0]).astype(jnp.float32)
    onehot = (my_slide[:, None] == jnp.arange(group_slides, dtype=jnp.int32)[None, :]).astype(
        jnp.float32
    ) * live[:, None]

    pooled, pull = jax.vjp(lambda p: block_pooled(p, my_pixels), params)
    slide_part = jnp.dot(onehot.T, pooled.T, precision=highest)
    placed = lax.dynamic_update_slice_in_dim(
        jnp.zeros((group_slides,), jnp.float32),
        jnp.where(chan == 0, target, 0.0),
        tile * slide_dev,
        axis=0,
    )
    slide_pack = jnp.concatenate(
        [slide_part, jnp.sum(onehot, axis=0)[:, None], placed[:, None]], axis=1
    )
    slide_pack = psum_steps(slide_pack, (("chan", "tx"), "tz"))
    width = slide_part.shape[1]
    sums = slide_pack[:, :width]
    counts = jnp.maximum(slide_pack[:, width], 1.0)
    target_all = slide_pack[:, width + 1]

    slide_feat = sums / counts[:, None]
    logit = jnp.dot(slide_feat, head, precision=highest)
    error = logit - target_all
    loss_part = 0.5 * jnp.sum(error * error) / all_slides
    d_logit = error / all_slides
    g_head = jnp.dot(slide_feat.T, d_logit, precision=highest)
    d_sums = d_logit[:, None] * head[None, :] / counts[:, None]
    d_pooled = jnp.dot(onehot, d_sums, precision=highest).T
    grads = pull(d_pooled)[0]

    lead = tile == 0
    g_head = jnp.where(lead & (chan == 0), g_head, 0.0)
    flat = jnp.concatenate(
        [g.reshape(chan_count, -1) for g in grads] + [g_head.reshape(chan_count, -1)], axis=1
    )
    dp_count = lax.psum(1, "dp")
    flat = jnp.concatenate(
        [flat, jnp.where(lead & (chan == 0), loss_part, 0.0) * jnp.ones((chan_count, 1))], axis=1
    )
    flat = jnp.broadcast_to(flat[None], (dp_count,) + flat.shape).reshape(-1, flat.shape[1])
    mine = scatter_sum(flat, ("dp", "chan"))
    mine = psum_steps(mine, ("tx", "tz"))

    outs = []
    offset = 0
    for s in shards[:10] + shards[10:]:
        n = s.size
        outs.append(mine[offset : offset + n].reshape(s.shape))
        offset += n
    outs.append(mine[offset])
    return tuple(outs)


def solution(mesh):
    devices = np.asarray(mesh.devices)
    dp, tiles, chan = devices.shape
    grid = Mesh(devices.reshape(dp, X_SPAN, tiles // X_SPAN, chan), ("dp", "tx", "tz", "chan"))
    rows = ("dp", "tx", "tz")
    in_specs = (
        P(None, rows),
        P(rows),
        P(rows),
        P("chan", None),
        P("chan"),
        P("chan", None),
        P("chan"),
        P("chan"),
        P("chan"),
        P("chan", None),
        P("chan"),
        P("chan", None),
        P("chan"),
        P("chan"),
        P(rows),
    )
    out_specs = (
        P("chan", None),
        P("chan"),
        P("chan", None),
        P("chan"),
        P("chan"),
        P("chan"),
        P("chan", None),
        P("chan"),
        P("chan", None),
        P("chan"),
        P("chan"),
        P(),
    )
    return jax.shard_map(
        per_device, mesh=grid, in_specs=in_specs, out_specs=out_specs, check_vma=False
    )
```

```python
import jax
import jax.numpy as jnp
import numpy as np
from jax import lax
from jax.sharding import Mesh
from jax.sharding import PartitionSpec as P

SIDE = 8
X_SPAN = 4
LANES = 128


epsilon = 1e-06
highest = lax.Precision.HIGHEST


def depthwise(stem_grid, kernel, bias):
    side_len = stem_grid.shape[-1]
    padded = jnp.pad(stem_grid, ((0, 0), (0, 0), (3, 3), (3, 3)))
    total = jnp.zeros_like(stem_grid)
    for kernel_row in range(7):
        for kernel_col in range(7):
            weight_tap = kernel[:, kernel_row * 7 + kernel_col][:, None, None, None]
            total = (
                total
                + weight_tap
                * padded[
                    :, :, kernel_row : kernel_row + side_len, kernel_col : kernel_col + side_len
                ]
            )
    return total + bias[:, None, None, None]


def block_pooled(params, pixels):
    w_patch, b_patch, dw_kernel, dw_bias, gain, shift, w_up, b_up, w_down, b_down = params
    width = w_patch.shape[0]
    tile_num = pixels.shape[1] // (SIDE * SIDE)
    stem = jnp.dot(w_patch, pixels, precision=highest) + b_patch[:, None]
    mixed = depthwise(stem.reshape(width, tile_num, SIDE, SIDE), dw_kernel, dw_bias).reshape(
        width, -1
    )
    average_value = jnp.mean(mixed, axis=0)
    variance = jnp.mean(mixed * mixed, axis=0) - average_value * average_value
    normed = (mixed - average_value) * lax.rsqrt(variance + epsilon) * gain[:, None] + shift[
        :, None
    ]
    pre_act = jnp.dot(w_up, normed, precision=highest) + b_up[:, None]
    hidden = jax.nn.gelu(pre_act, approximate=False)
    features = stem + jnp.dot(w_down.T, hidden, precision=highest) + b_down[:, None]
    return jnp.mean(features.reshape(width, tile_num, SIDE * SIDE), axis=2)


def spread_sum(value, axis):
    count = lax.psum(1, axis)
    copies = jnp.broadcast_to(value[None], (count,) + value.shape)
    return jnp.sum(lax.all_to_all(copies, axis, 0, 0, tiled=True), axis=0)


def psum_steps(value, axes):
    for axis in axes:
        value = spread_sum(value, axis)
    return value


def scatter_sum(value, axis):
    return jnp.sum(lax.all_to_all(value, axis, 0, 0, tiled=True), axis=0)


def pack(mats, vecs):
    blocks = [jnp.pad(m, ((0, 0), (0, 0), (0, LANES - m.shape[2]))) for m in mats]
    rows = jnp.stack([jnp.pad(v, ((0, 0), (0, LANES - v.shape[1]))) for v in vecs], axis=1)
    extra = (-rows.shape[1]) % 8
    rows = jnp.pad(rows, ((0, 0), (0, extra), (0, 0)))
    return jnp.concatenate(blocks + [rows], axis=1)


def unpack(block, mat_shapes, vec_sizes):
    mats = []
    offset = 0
    for r, m in mat_shapes:
        mats.append(block[..., offset : offset + r, :m])
        offset += r
    vecs = [block[..., offset + i, :n] for i, n in enumerate(vec_sizes)]
    return mats, vecs


def per_device(
    pixels,
    tile_slide,
    tile_count,
    w_patch,
    b_patch,
    dw_kernel,
    dw_bias,
    layernorm_gain,
    layernorm_bias,
    w_up,
    b_up,
    w_down,
    b_down,
    w_head,
    target,
):
    chan_count = lax.axis_size("chan")
    chan = lax.axis_index("chan")
    tile = lax.axis_index("tx") * lax.axis_size("tz") + lax.axis_index("tz")
    slot_count = tile_slide.shape[0]
    slots = slot_count // chan_count
    area = SIDE * SIDE
    slide_dev = target.shape[0]
    group_slides = slide_dev * lax.axis_size("tx") * lax.axis_size("tz")
    all_slides = group_slides * lax.axis_size("dp")

    mats = (w_patch, dw_kernel, w_up, w_down)
    vecs = (b_patch, dw_bias, layernorm_gain, layernorm_bias, b_up, b_down, w_head)
    mat_shapes = [m.shape for m in mats]
    vec_sizes = [v.shape[0] for v in vecs]
    packed = pack([m[None] for m in mats], [v[None] for v in vecs])
    copies = jnp.broadcast_to(packed, (chan_count,) + packed.shape[1:])
    gathered = lax.all_to_all(copies, "chan", 0, 0, tiled=True)
    full_mats, full_vecs = unpack(gathered, mat_shapes, vec_sizes)
    full_mats = [m.reshape(chan_count * r, c) for m, (r, c) in zip(full_mats, mat_shapes)]
    full_vecs = [v.reshape(-1) for v in full_vecs]
    params = (
        full_mats[0],
        full_vecs[0],
        full_mats[1],
        full_vecs[1],
        full_vecs[2],
        full_vecs[3],
        full_mats[2],
        full_vecs[4],
        full_mats[3],
        full_vecs[5],
    )
    head = full_vecs[6]

    my_pixels = lax.dynamic_slice_in_dim(pixels, chan * slots * area, slots * area, axis=1)
    my_slide = lax.dynamic_slice_in_dim(tile_slide, chan * slots, slots)
    slot_index = chan * slots + jnp.arange(slots, dtype=jnp.int32)
    live = (slot_index < tile_count[0]).astype(jnp.float32)
    onehot = (my_slide[:, None] == jnp.arange(group_slides, dtype=jnp.int32)[None, :]).astype(
        jnp.float32
    ) * live[:, None]

    pooled, pull = jax.vjp(lambda p: block_pooled(p, my_pixels), params)
    slide_part = jnp.dot(onehot.T, pooled.T, precision=highest)
    placed = lax.dynamic_update_slice_in_dim(
        jnp.zeros((group_slides,), jnp.float32),
        jnp.where(chan == 0, target, 0.0),
        tile * slide_dev,
        axis=0,
    )
    slide_pack = jnp.concatenate(
        [slide_part, jnp.sum(onehot, axis=0)[:, None], placed[:, None]], axis=1
    )
    slide_pack = psum_steps(slide_pack, (("chan", "tx"), "tz"))
    width = slide_part.shape[1]
    sums = slide_pack[:, :width]
    counts = jnp.maximum(slide_pack[:, width], 1.0)
    target_all = slide_pack[:, width + 1]

    slide_feat = sums / counts[:, None]
    logit = jnp.dot(slide_feat, head, precision=highest)
    error = logit - target_all
    loss_part = 0.5 * jnp.sum(error * error) / all_slides
    d_logit = error / all_slides
    g_head = jnp.dot(slide_feat.T, d_logit, precision=highest)
    d_sums = d_logit[:, None] * head[None, :] / counts[:, None]
    d_pooled = jnp.dot(onehot, d_sums, precision=highest).T
    grads = pull(d_pooled)[0]

    lead = (tile == 0) & (chan == 0)
    g_patch, g_bpatch, g_kernel, g_dwbias, g_gain, g_shift, g_up, g_bup, g_down, g_bdown = grads
    g_mats = [g.reshape(chan_count, -1, g.shape[1]) for g in (g_patch, g_kernel, g_up, g_down)]
    g_vecs = [
        g.reshape(chan_count, -1)
        for g in (g_bpatch, g_dwbias, g_gain, g_shift, g_bup, g_bdown, jnp.where(lead, g_head, 0.0))
    ]
    g_vecs.append(jnp.broadcast_to(jnp.where(lead, loss_part, 0.0), (chan_count, 1)))
    flat = pack(g_mats, g_vecs)
    dp_count = lax.psum(1, "dp")
    flat = jnp.broadcast_to(flat[None], (dp_count,) + flat.shape).reshape((-1,) + flat.shape[1:])
    mine = scatter_sum(flat, ("dp", "chan"))
    mine = psum_steps(mine, ("tx", "tz"))
    out_mats, out_vecs = unpack(mine, mat_shapes, vec_sizes + [1])
    outs = [
        out_mats[0],
        out_vecs[0],
        out_mats[1],
        out_vecs[1],
        out_vecs[2],
        out_vecs[3],
        out_mats[2],
        out_vecs[4],
        out_mats[3],
        out_vecs[5],
        out_vecs[6],
        out_vecs[7][0],
    ]
    return tuple(outs)


def solution(mesh):
    devices = np.asarray(mesh.devices)
    dp, tiles, chan = devices.shape
    grid = Mesh(devices.reshape(dp, X_SPAN, tiles // X_SPAN, chan), ("dp", "tx", "tz", "chan"))
    rows = ("dp", "tx", "tz")
    in_specs = (
        P(None, rows),
        P(rows),
        P(rows),
        P("chan", None),
        P("chan"),
        P("chan", None),
        P("chan"),
        P("chan"),
        P("chan"),
        P("chan", None),
        P("chan"),
        P("chan", None),
        P("chan"),
        P("chan"),
        P(rows),
    )
    out_specs = (
        P("chan", None),
        P("chan"),
        P("chan", None),
        P("chan"),
        P("chan"),
        P("chan"),
        P("chan", None),
        P("chan"),
        P("chan", None),
        P("chan"),
        P("chan"),
        P(),
    )
    return jax.shard_map(
        per_device, mesh=grid, in_specs=in_specs, out_specs=out_specs, check_vma=False
    )
```

```python
import jax
import jax.numpy as jnp
import numpy as np
from jax import lax
from jax.sharding import Mesh
from jax.sharding import PartitionSpec as P

SIDE = 8
X_SPAN = 4


epsilon = 1e-06
highest = lax.Precision.HIGHEST


def depthwise(stem_grid, kernel, bias):
    side_len = stem_grid.shape[-1]
    padded = jnp.pad(stem_grid, ((0, 0), (0, 0), (3, 3), (3, 3)))
    total = jnp.zeros_like(stem_grid)
    for kernel_row in range(7):
        for kernel_col in range(7):
            weight_tap = kernel[:, kernel_row * 7 + kernel_col][:, None, None, None]
            total = (
                total
                + weight_tap
                * padded[
                    :, :, kernel_row : kernel_row + side_len, kernel_col : kernel_col + side_len
                ]
            )
    return total + bias[:, None, None, None]


def block_pooled(params, pixels):
    w_patch, b_patch, dw_kernel, dw_bias, gain, shift, w_up, b_up, w_down, b_down = params
    width = w_patch.shape[0]
    tile_num = pixels.shape[1] // (SIDE * SIDE)
    stem = jnp.dot(w_patch, pixels, precision=highest) + b_patch[:, None]
    mixed = depthwise(stem.reshape(width, tile_num, SIDE, SIDE), dw_kernel, dw_bias).reshape(
        width, -1
    )
    average_value = jnp.mean(mixed, axis=0)
    variance = jnp.mean(mixed * mixed, axis=0) - average_value * average_value
    normed = (mixed - average_value) * lax.rsqrt(variance + epsilon) * gain[:, None] + shift[
        :, None
    ]
    pre_act = jnp.dot(w_up, normed, precision=highest) + b_up[:, None]
    hidden = jax.nn.gelu(pre_act, approximate=False)
    features = stem + jnp.dot(w_down.T, hidden, precision=highest) + b_down[:, None]
    return jnp.mean(features.reshape(width, tile_num, SIDE * SIDE), axis=2)


def spread_sum(value, axis):
    count = lax.psum(1, axis)
    copies = jnp.broadcast_to(value[None], (count,) + value.shape)
    return jnp.sum(lax.all_to_all(copies, axis, 0, 0, tiled=True), axis=0)


def gather_rows(value, axis):
    count = lax.psum(1, axis)
    copies = jnp.broadcast_to(value[None], (count,) + value.shape)
    return lax.all_to_all(copies, axis, 0, 0, tiled=True).reshape((-1,) + value.shape[1:])


def psum_steps(value, axes):
    for axis in axes:
        value = spread_sum(value, axis)
    return value


def scatter_sum(value, axis):
    return jnp.sum(lax.all_to_all(value, axis, 0, 0, tiled=True), axis=0)


def gather_chan(shards, chan_count, spread):
    packed = jnp.concatenate([s.reshape(1, -1) for s in shards], axis=1)
    if spread:
        copies = jnp.broadcast_to(packed, (chan_count, packed.shape[1]))
        gathered = lax.all_to_all(copies, "chan", 0, 0, tiled=True)
    else:
        gathered = lax.all_gather(packed, "chan", axis=0, tiled=True)
    full = []
    offset = 0
    for s in shards:
        n = s.size
        full.append(
            gathered[:, offset : offset + n].reshape((chan_count * s.shape[0],) + s.shape[1:])
        )
        offset += n
    return tuple(full)


def per_device(
    pixels,
    tile_slide,
    tile_count,
    w_patch,
    b_patch,
    dw_kernel,
    dw_bias,
    layernorm_gain,
    layernorm_bias,
    w_up,
    b_up,
    w_down,
    b_down,
    w_head,
    target,
):
    chan_count = lax.axis_size("chan")
    chan = lax.axis_index("chan")
    tile = lax.axis_index("tx") * lax.axis_size("tz") + lax.axis_index("tz")
    slot_count = tile_slide.shape[0]
    slots = slot_count // chan_count
    area = SIDE * SIDE
    slide_dev = target.shape[0]
    group_slides = slide_dev * lax.axis_size("tx") * lax.axis_size("tz")
    all_slides = group_slides * lax.axis_size("dp")

    shards = (
        w_patch,
        b_patch,
        dw_kernel,
        dw_bias,
        layernorm_gain,
        layernorm_bias,
        w_up,
        b_up,
        w_down,
        b_down,
        w_head,
    )
    full = gather_chan(shards, chan_count, spread=True)
    params = tuple(full[:10])
    head = full[10]

    my_pixels = lax.dynamic_slice_in_dim(pixels, chan * slots * area, slots * area, axis=1)
    my_slide = lax.dynamic_slice_in_dim(tile_slide, chan * slots, slots)
    slot_index = chan * slots + jnp.arange(slots, dtype=jnp.int32)
    live = (slot_index < tile_count[0]).astype(jnp.float32)
    onehot = (my_slide[:, None] == jnp.arange(group_slides, dtype=jnp.int32)[None, :]).astype(
        jnp.float32
    ) * live[:, None]

    pooled, pull = jax.vjp(lambda p: block_pooled(p, my_pixels), params)
    target_rows = jnp.zeros((slots,), jnp.float32)
    target_rows = lax.dynamic_update_slice_in_dim(target_rows, target, 0, axis=0)
    rows = jnp.concatenate(
        [
            pooled.T,
            my_slide.astype(jnp.float32)[:, None],
            live[:, None],
            jnp.where(chan == 0, target_rows, 0.0)[:, None],
        ],
        axis=1,
    )
    rows = gather_rows(gather_rows(rows, ("chan", "tx")), "tz")
    width = pooled.shape[0]
    onehot_all = (
        rows[:, width : width + 1] == jnp.arange(group_slides, dtype=jnp.float32)[None, :]
    ).astype(jnp.float32) * rows[:, width + 1 : width + 2]
    sums = jnp.dot(onehot_all.T, rows[:, :width], precision=highest)
    counts = jnp.maximum(jnp.sum(onehot_all, axis=0), 1.0)
    x_count = lax.psum(1, "tx")
    z_count = lax.psum(1, "tz")
    tile_of = np.arange(group_slides) // slide_dev
    where = (tile_of % z_count) * (rows.shape[0] // z_count) + (tile_of // z_count) * slots + (
        np.arange(group_slides) % slide_dev
    )
    target_all = rows[where, width + 2]

    slide_feat = sums / counts[:, None]
    logit = jnp.dot(slide_feat, head, precision=highest)
    error = logit - target_all
    loss_part = 0.5 * jnp.sum(error * error) / all_slides
    d_logit = error / all_slides
    g_head = jnp.dot(slide_feat.T, d_logit, precision=highest)
    d_sums = d_logit[:, None] * head[None, :] / counts[:, None]
    d_pooled = jnp.dot(onehot, d_sums, precision=highest).T
    grads = pull(d_pooled)[0]

    lead = tile == 0
    g_head = jnp.where(lead & (chan == 0), g_head, 0.0)
    flat = jnp.concatenate(
        [g.reshape(chan_count, -1) for g in grads] + [g_head.reshape(chan_count, -1)], axis=1
    )
    dp_count = lax.psum(1, "dp")
    flat = jnp.concatenate(
        [flat, jnp.where(lead & (chan == 0), loss_part, 0.0) * jnp.ones((chan_count, 1))], axis=1
    )
    flat = jnp.broadcast_to(flat[None], (dp_count,) + flat.shape).reshape(-1, flat.shape[1])
    mine = scatter_sum(flat, ("dp", "chan"))
    mine = psum_steps(mine, ("tx", "tz"))

    outs = []
    offset = 0
    for s in shards[:10] + shards[10:]:
        n = s.size
        outs.append(mine[offset : offset + n].reshape(s.shape))
        offset += n
    outs.append(mine[offset])
    return tuple(outs)


def solution(mesh):
    devices = np.asarray(mesh.devices)
    dp, tiles, chan = devices.shape
    grid = Mesh(devices.reshape(dp, X_SPAN, tiles // X_SPAN, chan), ("dp", "tx", "tz", "chan"))
    rows = ("dp", "tx", "tz")
    in_specs = (
        P(None, rows),
        P(rows),
        P(rows),
        P("chan", None),
        P("chan"),
        P("chan", None),
        P("chan"),
        P("chan"),
        P("chan"),
        P("chan", None),
        P("chan"),
        P("chan", None),
        P("chan"),
        P("chan"),
        P(rows),
    )
    out_specs = (
        P("chan", None),
        P("chan"),
        P("chan", None),
        P("chan"),
        P("chan"),
        P("chan"),
        P("chan", None),
        P("chan"),
        P("chan", None),
        P("chan"),
        P("chan"),
        P(),
    )
    return jax.shard_map(
        per_device, mesh=grid, in_specs=in_specs, out_specs=out_specs, check_vma=False
    )
```

```python
import jax
import jax.numpy as jnp
import numpy as np
from jax import lax
from jax.sharding import Mesh
from jax.sharding import PartitionSpec as P

SIDE = 8
X_SPAN = 4
MAT = (0, 2, 6, 8, 7)
SMALL = (1, 3, 4, 5, 9, 10)


epsilon = 1e-06
highest = lax.Precision.HIGHEST


def depthwise(stem_grid, kernel, bias):
    side_len = stem_grid.shape[-1]
    padded = jnp.pad(stem_grid, ((0, 0), (0, 0), (3, 3), (3, 3)))
    total = jnp.zeros_like(stem_grid)
    for kernel_row in range(7):
        for kernel_col in range(7):
            weight_tap = kernel[:, kernel_row * 7 + kernel_col][:, None, None, None]
            total = (
                total
                + weight_tap
                * padded[
                    :, :, kernel_row : kernel_row + side_len, kernel_col : kernel_col + side_len
                ]
            )
    return total + bias[:, None, None, None]


def block_pooled(params, pixels):
    w_patch, b_patch, dw_kernel, dw_bias, gain, shift, w_up, b_up, w_down, b_down = params
    width = w_patch.shape[0]
    tile_num = pixels.shape[1] // (SIDE * SIDE)
    stem = jnp.dot(w_patch, pixels, precision=highest) + b_patch[:, None]
    mixed = depthwise(stem.reshape(width, tile_num, SIDE, SIDE), dw_kernel, dw_bias).reshape(
        width, -1
    )
    average_value = jnp.mean(mixed, axis=0)
    variance = jnp.mean(mixed * mixed, axis=0) - average_value * average_value
    normed = (mixed - average_value) * lax.rsqrt(variance + epsilon) * gain[:, None] + shift[
        :, None
    ]
    pre_act = jnp.dot(w_up, normed, precision=highest) + b_up[:, None]
    hidden = jax.nn.gelu(pre_act, approximate=False)
    features = stem + jnp.dot(w_down.T, hidden, precision=highest) + b_down[:, None]
    return jnp.mean(features.reshape(width, tile_num, SIDE * SIDE), axis=2)


def spread_sum(value, axis):
    count = lax.psum(1, axis)
    copies = jnp.broadcast_to(value[None], (count,) + value.shape)
    return jnp.sum(lax.all_to_all(copies, axis, 0, 0, tiled=True), axis=0)


def gather_rows(value, axis):
    count = lax.psum(1, axis)
    copies = jnp.broadcast_to(value[None], (count,) + value.shape)
    return lax.all_to_all(copies, axis, 0, 0, tiled=True).reshape((-1,) + value.shape[1:])


def psum_steps(value, axes):
    for axis in axes:
        value = spread_sum(value, axis)
    return value


def scatter_sum(value, axis):
    return jnp.sum(lax.all_to_all(value, axis, 0, 0, tiled=True), axis=0)


def gather_chan(shards, chan_count, spread):
    packed = jnp.concatenate([s.reshape(1, -1) for s in shards], axis=1)
    if spread:
        copies = jnp.broadcast_to(packed, (chan_count, packed.shape[1]))
        gathered = lax.all_to_all(copies, "chan", 0, 0, tiled=True)
    else:
        gathered = lax.all_gather(packed, "chan", axis=0, tiled=True)
    full = []
    offset = 0
    for s in shards:
        n = s.size
        full.append(
            gathered[:, offset : offset + n].reshape((chan_count * s.shape[0],) + s.shape[1:])
        )
        offset += n
    return tuple(full)


def per_device(
    pixels,
    tile_slide,
    tile_count,
    w_patch,
    b_patch,
    dw_kernel,
    dw_bias,
    layernorm_gain,
    layernorm_bias,
    w_up,
    b_up,
    w_down,
    b_down,
    w_head,
    target,
):
    chan_count = lax.axis_size("chan")
    chan = lax.axis_index("chan")
    tile = lax.axis_index("tx") * lax.axis_size("tz") + lax.axis_index("tz")
    slot_count = tile_slide.shape[0]
    slots = slot_count // chan_count
    area = SIDE * SIDE
    slide_dev = target.shape[0]
    group_slides = slide_dev * lax.axis_size("tx") * lax.axis_size("tz")
    all_slides = group_slides * lax.axis_size("dp")

    shards = (
        w_patch,
        b_patch,
        dw_kernel,
        dw_bias,
        layernorm_gain,
        layernorm_bias,
        w_up,
        b_up,
        w_down,
        b_down,
        w_head,
    )
    packed = jnp.concatenate(
        [shards[i].reshape(1, -1) for i in MAT]
        + [jnp.stack([shards[i] for i in SMALL]).reshape(1, -1)],
        axis=1,
    )
    copies = jnp.broadcast_to(packed, (chan_count, packed.shape[1]))
    gathered = lax.all_to_all(copies, "chan", 0, 0, tiled=True)
    full = [None] * len(shards)
    offset = 0
    for i in MAT:
        n = shards[i].size
        full[i] = gathered[:, offset : offset + n].reshape(
            (chan_count * shards[i].shape[0],) + shards[i].shape[1:]
        )
        offset += n
    piece = shards[SMALL[0]].shape[0]
    block = gathered[:, offset : offset + len(SMALL) * piece].reshape(chan_count, len(SMALL), piece)
    block = block.transpose(1, 0, 2).reshape(len(SMALL), chan_count * piece)
    for k, i in enumerate(SMALL):
        full[i] = block[k]
    params = tuple(full[:10])
    head = full[10]

    my_pixels = lax.dynamic_slice_in_dim(pixels, chan * slots * area, slots * area, axis=1)
    my_slide = lax.dynamic_slice_in_dim(tile_slide, chan * slots, slots)
    slot_index = chan * slots + jnp.arange(slots, dtype=jnp.int32)
    live = (slot_index < tile_count[0]).astype(jnp.float32)
    onehot = (my_slide[:, None] == jnp.arange(group_slides, dtype=jnp.int32)[None, :]).astype(
        jnp.float32
    ) * live[:, None]

    pooled, pull = jax.vjp(lambda p: block_pooled(p, my_pixels), params)
    target_rows = jnp.zeros((slots,), jnp.float32)
    target_rows = lax.dynamic_update_slice_in_dim(target_rows, target, 0, axis=0)
    rows = jnp.concatenate(
        [
            pooled.T,
            my_slide.astype(jnp.float32)[:, None],
            live[:, None],
            jnp.where(chan == 0, target_rows, 0.0)[:, None],
        ],
        axis=1,
    )
    rows = gather_rows(gather_rows(rows, ("chan", "tx")), "tz")
    width = pooled.shape[0]
    onehot_all = (
        rows[:, width : width + 1] == jnp.arange(group_slides, dtype=jnp.float32)[None, :]
    ).astype(jnp.float32) * rows[:, width + 1 : width + 2]
    sums = jnp.dot(onehot_all.T, rows[:, :width], precision=highest)
    counts = jnp.maximum(jnp.sum(onehot_all, axis=0), 1.0)
    x_count = lax.psum(1, "tx")
    z_count = lax.psum(1, "tz")
    tile_of = np.arange(group_slides) // slide_dev
    where = (tile_of % z_count) * (rows.shape[0] // z_count) + (tile_of // z_count) * slots + (
        np.arange(group_slides) % slide_dev
    )
    target_all = rows[where, width + 2]

    slide_feat = sums / counts[:, None]
    logit = jnp.dot(slide_feat, head, precision=highest)
    error = logit - target_all
    loss_part = 0.5 * jnp.sum(error * error) / all_slides
    d_logit = error / all_slides
    g_head = jnp.dot(slide_feat.T, d_logit, precision=highest)
    d_sums = d_logit[:, None] * head[None, :] / counts[:, None]
    d_pooled = jnp.dot(onehot, d_sums, precision=highest).T
    grads = pull(d_pooled)[0]

    lead = tile == 0
    g_head = jnp.where(lead & (chan == 0), g_head, 0.0)
    all_grads = list(grads) + [g_head]
    small = jnp.stack([all_grads[i] for i in SMALL]).reshape(len(SMALL), chan_count, -1)
    flat = jnp.concatenate(
        [all_grads[i].reshape(chan_count, -1) for i in MAT]
        + [small.transpose(1, 0, 2).reshape(chan_count, -1)],
        axis=1,
    )
    dp_count = lax.psum(1, "dp")
    flat = jnp.concatenate(
        [flat, jnp.where(lead & (chan == 0), loss_part, 0.0) * jnp.ones((chan_count, 1))], axis=1
    )
    flat = jnp.broadcast_to(flat[None], (dp_count,) + flat.shape).reshape(-1, flat.shape[1])
    mine = scatter_sum(flat, ("dp", "chan"))
    mine = psum_steps(mine, ("tx", "tz"))

    outs = [None] * len(shards)
    offset = 0
    for i in MAT:
        n = shards[i].size
        outs[i] = mine[offset : offset + n].reshape(shards[i].shape)
        offset += n
    block = mine[offset : offset + len(SMALL) * piece].reshape(len(SMALL), piece)
    for k, i in enumerate(SMALL):
        outs[i] = block[k]
    outs.append(mine[offset + len(SMALL) * piece])
    return tuple(outs)


def solution(mesh):
    devices = np.asarray(mesh.devices)
    dp, tiles, chan = devices.shape
    grid = Mesh(devices.reshape(dp, X_SPAN, tiles // X_SPAN, chan), ("dp", "tx", "tz", "chan"))
    rows = ("dp", "tx", "tz")
    in_specs = (
        P(None, rows),
        P(rows),
        P(rows),
        P("chan", None),
        P("chan"),
        P("chan", None),
        P("chan"),
        P("chan"),
        P("chan"),
        P("chan", None),
        P("chan"),
        P("chan", None),
        P("chan"),
        P("chan"),
        P(rows),
    )
    out_specs = (
        P("chan", None),
        P("chan"),
        P("chan", None),
        P("chan"),
        P("chan"),
        P("chan"),
        P("chan", None),
        P("chan"),
        P("chan", None),
        P("chan"),
        P("chan"),
        P(),
    )
    return jax.shard_map(
        per_device, mesh=grid, in_specs=in_specs, out_specs=out_specs, check_vma=False
    )
```

```python
import jax
import jax.numpy as jnp
import numpy as np
from jax import lax
from jax.sharding import Mesh
from jax.sharding import PartitionSpec as P

SIDE = 8
X_SPAN = 4


epsilon = 1e-06
highest = lax.Precision.HIGHEST


def depthwise(stem_grid, kernel, bias):
    side_len = stem_grid.shape[-1]
    padded = jnp.pad(stem_grid, ((0, 0), (0, 0), (3, 3), (3, 3)))
    total = jnp.zeros_like(stem_grid)
    for kernel_row in range(7):
        for kernel_col in range(7):
            weight_tap = kernel[:, kernel_row * 7 + kernel_col][:, None, None, None]
            total = (
                total
                + weight_tap
                * padded[
                    :, :, kernel_row : kernel_row + side_len, kernel_col : kernel_col + side_len
                ]
            )
    return total + bias[:, None, None, None]


def block_pooled(params, pixels):
    w_patch, b_patch, dw_kernel, dw_bias, gain, shift, w_up, b_up, w_down, b_down = params
    width = w_patch.shape[0]
    tile_num = pixels.shape[1] // (SIDE * SIDE)
    stem = jnp.dot(w_patch, pixels, precision=highest) + b_patch[:, None]
    mixed = depthwise(stem.reshape(width, tile_num, SIDE, SIDE), dw_kernel, dw_bias).reshape(
        width, -1
    )
    average_value = jnp.mean(mixed, axis=0)
    variance = jnp.mean(mixed * mixed, axis=0) - average_value * average_value
    normed = (mixed - average_value) * lax.rsqrt(variance + epsilon) * gain[:, None] + shift[
        :, None
    ]
    pre_act = jnp.dot(w_up, normed, precision=highest) + b_up[:, None]
    hidden = jax.nn.gelu(pre_act, approximate=False)
    features = stem + jnp.dot(w_down.T, hidden, precision=highest) + b_down[:, None]
    return jnp.mean(features.reshape(width, tile_num, SIDE * SIDE), axis=2)


def spread_sum(value, axis):
    count = lax.psum(1, axis)
    copies = jnp.broadcast_to(value[None], (count,) + value.shape)
    return jnp.sum(lax.all_to_all(copies, axis, 0, 0, tiled=True), axis=0)


def gather_rows(value, axis):
    count = lax.psum(1, axis)
    copies = jnp.broadcast_to(value[None], (count,) + value.shape)
    return lax.all_to_all(copies, axis, 0, 0, tiled=True).reshape((-1,) + value.shape[1:])


def psum_steps(value, axes):
    for axis in axes:
        value = spread_sum(value, axis)
    return value


def scatter_sum(value, axis):
    return jnp.sum(lax.all_to_all(value, axis, 0, 0, tiled=True), axis=0)


def gather_chan(shards, chan_count, spread):
    packed = jnp.concatenate([s.reshape(1, -1) for s in shards], axis=1)
    if spread:
        copies = jnp.broadcast_to(packed, (chan_count, packed.shape[1]))
        gathered = lax.all_to_all(copies, "chan", 0, 0, tiled=True)
    else:
        gathered = lax.all_gather(packed, "chan", axis=0, tiled=True)
    full = []
    offset = 0
    for s in shards:
        n = s.size
        full.append(
            gathered[:, offset : offset + n].reshape((chan_count * s.shape[0],) + s.shape[1:])
        )
        offset += n
    return tuple(full)


def per_device(
    pixels,
    tile_slide,
    tile_count,
    w_patch,
    b_patch,
    dw_kernel,
    dw_bias,
    layernorm_gain,
    layernorm_bias,
    w_up,
    b_up,
    w_down,
    b_down,
    w_head,
    target,
):
    chan_count = lax.axis_size("chan")
    chan = lax.axis_index("chan")
    tile = lax.axis_index("tx") * lax.axis_size("tz") + lax.axis_index("tz")
    slot_count = tile_slide.shape[0]
    slots = slot_count // chan_count
    area = SIDE * SIDE
    slide_dev = target.shape[0]
    group_slides = slide_dev * lax.axis_size("tx") * lax.axis_size("tz")
    all_slides = group_slides * lax.axis_size("dp")

    shards = (
        w_patch,
        b_patch,
        dw_kernel,
        dw_bias,
        layernorm_gain,
        layernorm_bias,
        w_up,
        b_up,
        w_down,
        b_down,
        w_head,
    )
    full = gather_chan(shards, chan_count, spread=True)
    params = tuple(full[:10])
    head = full[10]

    my_pixels = lax.dynamic_slice_in_dim(pixels, chan * slots * area, slots * area, axis=1)
    my_slide = lax.dynamic_slice_in_dim(tile_slide, chan * slots, slots)
    slot_index = chan * slots + jnp.arange(slots, dtype=jnp.int32)
    live = (slot_index < tile_count[0]).astype(jnp.float32)
    onehot = (my_slide[:, None] == jnp.arange(group_slides, dtype=jnp.int32)[None, :]).astype(
        jnp.float32
    ) * live[:, None]

    pooled, pull = jax.vjp(lambda p: block_pooled(p, my_pixels), params)
    target_rows = jnp.zeros((slots,), jnp.float32)
    target_rows = lax.dynamic_update_slice_in_dim(target_rows, target, 0, axis=0)
    rows = jnp.concatenate(
        [
            pooled.T,
            my_slide.astype(jnp.float32)[:, None],
            live[:, None],
            jnp.where(chan == 0, target_rows, 0.0)[:, None],
        ],
        axis=1,
    )
    rows = gather_rows(gather_rows(rows, "tz"), ("chan", "tx"))
    width = pooled.shape[0]
    onehot_all = (
        rows[:, width : width + 1] == jnp.arange(group_slides, dtype=jnp.float32)[None, :]
    ).astype(jnp.float32) * rows[:, width + 1 : width + 2]
    sums = jnp.dot(onehot_all.T, rows[:, :width], precision=highest)
    counts = jnp.maximum(jnp.sum(onehot_all, axis=0), 1.0)
    z_count = lax.psum(1, "tz")
    tile_of = np.arange(group_slides) // slide_dev
    where = (tile_of // z_count) * (slots * z_count) + (tile_of % z_count) * slots + (
        np.arange(group_slides) % slide_dev
    )
    target_all = rows[where, width + 2]

    slide_feat = sums / counts[:, None]
    logit = jnp.dot(slide_feat, head, precision=highest)
    error = logit - target_all
    loss_part = 0.5 * jnp.sum(error * error) / all_slides
    d_logit = error / all_slides
    g_head = jnp.dot(slide_feat.T, d_logit, precision=highest)
    d_sums = d_logit[:, None] * head[None, :] / counts[:, None]
    d_pooled = jnp.dot(onehot, d_sums, precision=highest).T
    grads = pull(d_pooled)[0]

    lead = tile == 0
    g_head = jnp.where(lead & (chan == 0), g_head, 0.0)
    flat = jnp.concatenate(
        [g.reshape(chan_count, -1) for g in grads] + [g_head.reshape(chan_count, -1)], axis=1
    )
    dp_count = lax.psum(1, "dp")
    flat = jnp.concatenate(
        [flat, jnp.where(lead & (chan == 0), loss_part, 0.0) * jnp.ones((chan_count, 1))], axis=1
    )
    flat = jnp.broadcast_to(flat[None], (dp_count,) + flat.shape).reshape(-1, flat.shape[1])
    mine = scatter_sum(flat, ("dp", "chan"))
    mine = psum_steps(mine, ("tx", "tz"))

    outs = []
    offset = 0
    for s in shards[:10] + shards[10:]:
        n = s.size
        outs.append(mine[offset : offset + n].reshape(s.shape))
        offset += n
    outs.append(mine[offset])
    return tuple(outs)


def solution(mesh):
    devices = np.asarray(mesh.devices)
    dp, tiles, chan = devices.shape
    grid = Mesh(devices.reshape(dp, X_SPAN, tiles // X_SPAN, chan), ("dp", "tx", "tz", "chan"))
    rows = ("dp", "tx", "tz")
    in_specs = (
        P(None, rows),
        P(rows),
        P(rows),
        P("chan", None),
        P("chan"),
        P("chan", None),
        P("chan"),
        P("chan"),
        P("chan"),
        P("chan", None),
        P("chan"),
        P("chan", None),
        P("chan"),
        P("chan"),
        P(rows),
    )
    out_specs = (
        P("chan", None),
        P("chan"),
        P("chan", None),
        P("chan"),
        P("chan"),
        P("chan"),
        P("chan", None),
        P("chan"),
        P("chan", None),
        P("chan"),
        P("chan"),
        P(),
    )
    return jax.shard_map(
        per_device, mesh=grid, in_specs=in_specs, out_specs=out_specs, check_vma=False
    )
```

```python
import jax
import jax.numpy as jnp
import numpy as np
from jax import lax
from jax.sharding import Mesh
from jax.sharding import PartitionSpec as P

SIDE = 8
X_SPAN = 4


epsilon = 1e-06
highest = lax.Precision.HIGHEST


def depthwise(stem_grid, kernel, bias):
    side_len = stem_grid.shape[-1]
    padded = jnp.pad(stem_grid, ((0, 0), (0, 0), (3, 3), (3, 3)))
    total = jnp.zeros_like(stem_grid)
    for kernel_row in range(7):
        for kernel_col in range(7):
            weight_tap = kernel[:, kernel_row * 7 + kernel_col][:, None, None, None]
            total = (
                total
                + weight_tap
                * padded[
                    :, :, kernel_row : kernel_row + side_len, kernel_col : kernel_col + side_len
                ]
            )
    return total + bias[:, None, None, None]


def block_pooled(params, pixels):
    w_patch, b_patch, dw_kernel, dw_bias, gain, shift, w_up, b_up, w_down, b_down = params
    width = w_patch.shape[0]
    tile_num = pixels.shape[1] // (SIDE * SIDE)
    stem = jnp.dot(w_patch, pixels, precision=highest) + b_patch[:, None]
    mixed = depthwise(stem.reshape(width, tile_num, SIDE, SIDE), dw_kernel, dw_bias).reshape(
        width, -1
    )
    average_value = jnp.mean(mixed, axis=0)
    variance = jnp.mean(mixed * mixed, axis=0) - average_value * average_value
    normed = (mixed - average_value) * lax.rsqrt(variance + epsilon) * gain[:, None] + shift[
        :, None
    ]
    pre_act = jnp.dot(w_up, normed, precision=highest) + b_up[:, None]
    hidden = jax.nn.gelu(pre_act, approximate=False)
    features = stem + jnp.dot(w_down.T, hidden, precision=highest) + b_down[:, None]
    return jnp.mean(features.reshape(width, tile_num, SIDE * SIDE), axis=2)


def spread_sum(value, axis):
    count = lax.psum(1, axis)
    copies = jnp.broadcast_to(value[None], (count,) + value.shape)
    return jnp.sum(lax.all_to_all(copies, axis, 0, 0, tiled=True), axis=0)


def gather_rows(value, axis):
    count = lax.psum(1, axis)
    copies = jnp.broadcast_to(value[None], (count,) + value.shape)
    return lax.all_to_all(copies, axis, 0, 0, tiled=True).reshape((-1,) + value.shape[1:])


def psum_steps(value, axes):
    for axis in axes:
        value = spread_sum(value, axis)
    return value


def scatter_sum(value, axis):
    return jnp.sum(lax.all_to_all(value, axis, 0, 0, tiled=True), axis=0)


def gather_chan(shards, chan_count, spread):
    packed = jnp.concatenate([s.reshape(1, -1) for s in shards], axis=1)
    if spread:
        copies = jnp.broadcast_to(packed, (chan_count, packed.shape[1]))
        gathered = lax.all_to_all(copies, "chan", 0, 0, tiled=True)
    else:
        gathered = lax.all_gather(packed, "chan", axis=0, tiled=True)
    full = []
    offset = 0
    for s in shards:
        n = s.size
        full.append(
            gathered[:, offset : offset + n].reshape((chan_count * s.shape[0],) + s.shape[1:])
        )
        offset += n
    return tuple(full)


def per_device(
    pixels,
    tile_slide,
    tile_count,
    w_patch,
    b_patch,
    dw_kernel,
    dw_bias,
    layernorm_gain,
    layernorm_bias,
    w_up,
    b_up,
    w_down,
    b_down,
    w_head,
    target,
):
    chan_count = lax.axis_size("chan")
    chan = lax.axis_index("chan")
    tile = lax.axis_index("tx") * lax.axis_size("tz") + lax.axis_index("tz")
    slot_count = tile_slide.shape[0]
    slots = slot_count // chan_count
    area = SIDE * SIDE
    slide_dev = target.shape[0]
    group_slides = slide_dev * lax.axis_size("tx") * lax.axis_size("tz")
    all_slides = group_slides * lax.axis_size("dp")

    shards = (
        w_patch,
        b_patch,
        dw_kernel,
        dw_bias,
        layernorm_gain,
        layernorm_bias,
        w_up,
        b_up,
        w_down,
        b_down,
        w_head,
    )
    full = gather_chan(shards, chan_count, spread=True)
    params = tuple(full[:10])
    head = full[10]

    my_pixels = lax.dynamic_slice_in_dim(pixels, chan * slots * area, slots * area, axis=1)
    my_slide = lax.dynamic_slice_in_dim(tile_slide, chan * slots, slots)
    slot_index = chan * slots + jnp.arange(slots, dtype=jnp.int32)
    live = (slot_index < tile_count[0]).astype(jnp.float32)
    onehot = (my_slide[:, None] == jnp.arange(group_slides, dtype=jnp.int32)[None, :]).astype(
        jnp.float32
    ) * live[:, None]

    pooled, pull = jax.vjp(lambda p: block_pooled(p, my_pixels), params)
    target_rows = jnp.zeros((slots,), jnp.float32)
    target_rows = lax.dynamic_update_slice_in_dim(target_rows, target, 0, axis=0)
    rows = jnp.concatenate(
        [
            pooled.T,
            my_slide.astype(jnp.float32)[:, None],
            live[:, None],
            jnp.where(chan == 0, target_rows, 0.0)[:, None],
        ],
        axis=1,
    )
    rows = gather_rows(gather_rows(rows, "tz"), ("chan", "tx"))
    width = pooled.shape[0]
    onehot_all = (
        rows[:, width : width + 1] == jnp.arange(group_slides, dtype=jnp.float32)[None, :]
    ).astype(jnp.float32) * rows[:, width + 1 : width + 2]
    sums = jnp.dot(onehot_all.T, rows[:, :width], precision=highest)
    counts = jnp.maximum(jnp.sum(onehot_all, axis=0), 1.0)
    z_count = lax.psum(1, "tz")
    tile_of = np.arange(group_slides) // slide_dev
    where = (tile_of // z_count) * (slots * z_count) + (tile_of % z_count) * slots + (
        np.arange(group_slides) % slide_dev
    )
    target_all = rows[where, width + 2]

    slide_feat = sums / counts[:, None]
    logit = jnp.dot(slide_feat, head, precision=highest)
    error = logit - target_all
    loss_part = 0.5 * jnp.sum(error * error) / all_slides
    d_logit = error / all_slides
    g_head = jnp.dot(slide_feat.T, d_logit, precision=highest)
    d_sums = d_logit[:, None] * head[None, :] / counts[:, None]
    d_pooled = jnp.dot(onehot, d_sums, precision=highest).T
    grads = pull(d_pooled)[0]

    lead = tile == 0
    g_head = jnp.where(lead & (chan == 0), g_head, 0.0)
    flat = jnp.concatenate(
        [g.reshape(chan_count, -1) for g in grads] + [g_head.reshape(chan_count, -1)], axis=1
    )
    dp_count = lax.psum(1, "dp")
    flat = jnp.concatenate(
        [flat, jnp.where(lead & (chan == 0), loss_part, 0.0) * jnp.ones((chan_count, 1))], axis=1
    )
    length = flat.shape[1]
    half = -(-length // dp_count)
    flat = jnp.pad(flat, ((0, 0), (0, half * dp_count - length)))
    flat = flat.reshape(chan_count, dp_count, half).transpose(1, 0, 2).reshape(-1, half)
    mine = scatter_sum(flat, ("dp", "chan"))
    mine = psum_steps(mine, ("tx", "tz"))
    mine = gather_rows(mine[None], "dp").reshape(-1)[:length]

    outs = []
    offset = 0
    for s in shards[:10] + shards[10:]:
        n = s.size
        outs.append(mine[offset : offset + n].reshape(s.shape))
        offset += n
    outs.append(mine[offset])
    return tuple(outs)


def solution(mesh):
    devices = np.asarray(mesh.devices)
    dp, tiles, chan = devices.shape
    grid = Mesh(devices.reshape(dp, X_SPAN, tiles // X_SPAN, chan), ("dp", "tx", "tz", "chan"))
    rows = ("dp", "tx", "tz")
    in_specs = (
        P(None, rows),
        P(rows),
        P(rows),
        P("chan", None),
        P("chan"),
        P("chan", None),
        P("chan"),
        P("chan"),
        P("chan"),
        P("chan", None),
        P("chan"),
        P("chan", None),
        P("chan"),
        P("chan"),
        P(rows),
    )
    out_specs = (
        P("chan", None),
        P("chan"),
        P("chan", None),
        P("chan"),
        P("chan"),
        P("chan"),
        P("chan", None),
        P("chan"),
        P("chan", None),
        P("chan"),
        P("chan"),
        P(),
    )
    return jax.shard_map(
        per_device, mesh=grid, in_specs=in_specs, out_specs=out_specs, check_vma=False
    )
```

```python
import jax
import jax.numpy as jnp
import numpy as np
from jax import lax
from jax.sharding import Mesh
from jax.sharding import PartitionSpec as P

SIDE = 8
X_SPAN = 4


epsilon = 1e-06
highest = lax.Precision.HIGHEST


def depthwise(stem_grid, kernel, bias):
    side_len = stem_grid.shape[-1]
    padded = jnp.pad(stem_grid, ((0, 0), (0, 0), (3, 3), (3, 3)))
    total = jnp.zeros_like(stem_grid)
    for kernel_row in range(7):
        for kernel_col in range(7):
            weight_tap = kernel[:, kernel_row * 7 + kernel_col][:, None, None, None]
            total = (
                total
                + weight_tap
                * padded[
                    :, :, kernel_row : kernel_row + side_len, kernel_col : kernel_col + side_len
                ]
            )
    return total + bias[:, None, None, None]


def block_pooled(params, pixels):
    w_patch, b_patch, dw_kernel, dw_bias, gain, shift, w_up, b_up, w_down, b_down = params
    width = w_patch.shape[0]
    tile_num = pixels.shape[1] // (SIDE * SIDE)
    stem = jnp.dot(w_patch, pixels, precision=highest) + b_patch[:, None]
    mixed = depthwise(stem.reshape(width, tile_num, SIDE, SIDE), dw_kernel, dw_bias).reshape(
        width, -1
    )
    average_value = jnp.mean(mixed, axis=0)
    variance = jnp.mean(mixed * mixed, axis=0) - average_value * average_value
    normed = (mixed - average_value) * lax.rsqrt(variance + epsilon) * gain[:, None] + shift[
        :, None
    ]
    pre_act = jnp.dot(w_up, normed, precision=highest) + b_up[:, None]
    hidden = jax.nn.gelu(pre_act, approximate=False)
    features = stem + jnp.dot(w_down.T, hidden, precision=highest) + b_down[:, None]
    return jnp.mean(features.reshape(width, tile_num, SIDE * SIDE), axis=2)


def spread_sum(value, axis):
    count = lax.psum(1, axis)
    copies = jnp.broadcast_to(value[None], (count,) + value.shape)
    return jnp.sum(lax.all_to_all(copies, axis, 0, 0, tiled=True), axis=0)


def gather_rows(value, axis):
    count = lax.psum(1, axis)
    copies = jnp.broadcast_to(value[None], (count,) + value.shape)
    return lax.all_to_all(copies, axis, 0, 0, tiled=True).reshape((-1,) + value.shape[1:])


def psum_steps(value, axes):
    for axis in axes:
        value = spread_sum(value, axis)
    return value


def scatter_sum(value, axis):
    return jnp.sum(lax.all_to_all(value, axis, 0, 0, tiled=True), axis=0)


def gather_chan(shards, chan_count, spread):
    packed = jnp.concatenate([s.reshape(1, -1) for s in shards], axis=1)
    if spread:
        copies = jnp.broadcast_to(packed, (chan_count, packed.shape[1]))
        gathered = lax.all_to_all(copies, "chan", 0, 0, tiled=True)
    else:
        gathered = lax.all_gather(packed, "chan", axis=0, tiled=True)
    full = []
    offset = 0
    for s in shards:
        n = s.size
        full.append(
            gathered[:, offset : offset + n].reshape((chan_count * s.shape[0],) + s.shape[1:])
        )
        offset += n
    return tuple(full)


def per_device(
    pixels,
    tile_slide,
    tile_count,
    w_patch,
    b_patch,
    dw_kernel,
    dw_bias,
    layernorm_gain,
    layernorm_bias,
    w_up,
    b_up,
    w_down,
    b_down,
    w_head,
    target,
):
    chan_count = lax.axis_size("chan")
    chan = lax.axis_index("chan")
    tile = lax.axis_index("tx") * lax.axis_size("tz") + lax.axis_index("tz")
    slot_count = tile_slide.shape[0]
    slots = slot_count // chan_count
    area = SIDE * SIDE
    slide_dev = target.shape[0]
    group_slides = slide_dev * lax.axis_size("tx") * lax.axis_size("tz")
    all_slides = group_slides * lax.axis_size("dp")

    shards = (
        w_patch,
        b_patch,
        dw_kernel,
        dw_bias,
        layernorm_gain,
        layernorm_bias,
        w_up,
        b_up,
        w_down,
        b_down,
        w_head,
    )
    full = gather_chan(shards, chan_count, spread=True)
    params = tuple(full[:10])
    head = full[10]

    my_pixels = lax.dynamic_slice_in_dim(pixels, chan * slots * area, slots * area, axis=1)
    my_slide = lax.dynamic_slice_in_dim(tile_slide, chan * slots, slots)
    slot_index = chan * slots + jnp.arange(slots, dtype=jnp.int32)
    live = (slot_index < tile_count[0]).astype(jnp.float32)
    onehot = (my_slide[:, None] == jnp.arange(group_slides, dtype=jnp.int32)[None, :]).astype(
        jnp.float32
    ) * live[:, None]

    pooled, pull = jax.vjp(lambda p: block_pooled(p, my_pixels), params)
    target_rows = jnp.zeros((slots,), jnp.float32)
    target_rows = lax.dynamic_update_slice_in_dim(target_rows, target, 0, axis=0)
    rows = jnp.concatenate(
        [
            pooled.T,
            my_slide.astype(jnp.float32)[:, None],
            live[:, None],
            jnp.where(chan == 0, target_rows, 0.0)[:, None],
        ],
        axis=1,
    )
    rows = gather_rows(rows, ("chan", "tx", "tz"))
    width = pooled.shape[0]
    onehot_all = (
        rows[:, width : width + 1] == jnp.arange(group_slides, dtype=jnp.float32)[None, :]
    ).astype(jnp.float32) * rows[:, width + 1 : width + 2]
    sums = jnp.dot(onehot_all.T, rows[:, :width], precision=highest)
    counts = jnp.maximum(jnp.sum(onehot_all, axis=0), 1.0)
    tile_of = np.arange(group_slides) // slide_dev
    where = tile_of * slots + np.arange(group_slides) % slide_dev
    target_all = rows[where, width + 2]

    slide_feat = sums / counts[:, None]
    logit = jnp.dot(slide_feat, head, precision=highest)
    error = logit - target_all
    loss_part = 0.5 * jnp.sum(error * error) / all_slides
    d_logit = error / all_slides
    g_head = jnp.dot(slide_feat.T, d_logit, precision=highest)
    d_sums = d_logit[:, None] * head[None, :] / counts[:, None]
    d_pooled = jnp.dot(onehot, d_sums, precision=highest).T
    grads = pull(d_pooled)[0]

    lead = tile == 0
    g_head = jnp.where(lead & (chan == 0), g_head, 0.0)
    flat = jnp.concatenate(
        [g.reshape(chan_count, -1) for g in grads] + [g_head.reshape(chan_count, -1)], axis=1
    )
    dp_count = lax.psum(1, "dp")
    flat = jnp.concatenate(
        [flat, jnp.where(lead & (chan == 0), loss_part, 0.0) * jnp.ones((chan_count, 1))], axis=1
    )
    length = flat.shape[1]
    half = -(-length // dp_count)
    flat = jnp.pad(flat, ((0, 0), (0, half * dp_count - length)))
    flat = flat.reshape(chan_count, dp_count, half).transpose(1, 0, 2).reshape(-1, half)
    mine = scatter_sum(flat, ("dp", "chan"))
    mine = psum_steps(mine, ("tx", "tz"))
    mine = gather_rows(mine[None], "dp").reshape(-1)[:length]

    outs = []
    offset = 0
    for s in shards[:10] + shards[10:]:
        n = s.size
        outs.append(mine[offset : offset + n].reshape(s.shape))
        offset += n
    outs.append(mine[offset])
    return tuple(outs)


def solution(mesh):
    devices = np.asarray(mesh.devices)
    dp, tiles, chan = devices.shape
    grid = Mesh(devices.reshape(dp, X_SPAN, tiles // X_SPAN, chan), ("dp", "tx", "tz", "chan"))
    rows = ("dp", "tx", "tz")
    in_specs = (
        P(None, rows),
        P(rows),
        P(rows),
        P("chan", None),
        P("chan"),
        P("chan", None),
        P("chan"),
        P("chan"),
        P("chan"),
        P("chan", None),
        P("chan"),
        P("chan", None),
        P("chan"),
        P("chan"),
        P(rows),
    )
    out_specs = (
        P("chan", None),
        P("chan"),
        P("chan", None),
        P("chan"),
        P("chan"),
        P("chan"),
        P("chan", None),
        P("chan"),
        P("chan", None),
        P("chan"),
        P("chan"),
        P(),
    )
    return jax.shard_map(
        per_device, mesh=grid, in_specs=in_specs, out_specs=out_specs, check_vma=False
    )
```

```python
import jax
import jax.numpy as jnp
import numpy as np
from jax import lax
from jax.sharding import Mesh
from jax.sharding import PartitionSpec as P

SIDE = 8
X_SPAN = 4


epsilon = 1e-06
highest = lax.Precision.HIGHEST


def depthwise(stem_grid, kernel, bias):
    side_len = stem_grid.shape[-1]
    padded = jnp.pad(stem_grid, ((0, 0), (0, 0), (3, 3), (3, 3)))
    total = jnp.zeros_like(stem_grid)
    for kernel_row in range(7):
        for kernel_col in range(7):
            weight_tap = kernel[:, kernel_row * 7 + kernel_col][:, None, None, None]
            total = (
                total
                + weight_tap
                * padded[
                    :, :, kernel_row : kernel_row + side_len, kernel_col : kernel_col + side_len
                ]
            )
    return total + bias[:, None, None, None]


def block_pooled(params, pixels):
    w_patch, b_patch, dw_kernel, dw_bias, gain, shift, w_up, b_up, w_down, b_down = params
    width = w_patch.shape[0]
    tile_num = pixels.shape[1] // (SIDE * SIDE)
    stem = jnp.dot(w_patch, pixels, precision=highest) + b_patch[:, None]
    mixed = depthwise(stem.reshape(width, tile_num, SIDE, SIDE), dw_kernel, dw_bias).reshape(
        width, -1
    )
    average_value = jnp.mean(mixed, axis=0)
    variance = jnp.mean(mixed * mixed, axis=0) - average_value * average_value
    normed = (mixed - average_value) * lax.rsqrt(variance + epsilon) * gain[:, None] + shift[
        :, None
    ]
    pre_act = jnp.dot(w_up, normed, precision=highest) + b_up[:, None]
    hidden = jax.nn.gelu(pre_act, approximate=False)
    features = stem + jnp.dot(w_down.T, hidden, precision=highest) + b_down[:, None]
    return jnp.mean(features.reshape(width, tile_num, SIDE * SIDE), axis=2)


def spread_sum(value, axis):
    count = lax.psum(1, axis)
    copies = jnp.broadcast_to(value[None], (count,) + value.shape)
    return jnp.sum(lax.all_to_all(copies, axis, 0, 0, tiled=True), axis=0)


def gather_rows(value, axis):
    count = lax.psum(1, axis)
    copies = jnp.broadcast_to(value[None], (count,) + value.shape)
    return lax.all_to_all(copies, axis, 0, 0, tiled=True).reshape((-1,) + value.shape[1:])


def psum_steps(value, axes):
    for axis in axes:
        value = spread_sum(value, axis)
    return value


def scatter_sum(value, axis):
    return jnp.sum(lax.all_to_all(value, axis, 0, 0, tiled=True), axis=0)


def gather_chan(shards, chan_count, spread):
    packed = jnp.concatenate([s.reshape(1, -1) for s in shards], axis=1)
    if spread:
        copies = jnp.broadcast_to(packed, (chan_count, packed.shape[1]))
        gathered = lax.all_to_all(copies, "chan", 0, 0, tiled=True)
    else:
        gathered = lax.all_gather(packed, "chan", axis=0, tiled=True)
    full = []
    offset = 0
    for s in shards:
        n = s.size
        full.append(
            gathered[:, offset : offset + n].reshape((chan_count * s.shape[0],) + s.shape[1:])
        )
        offset += n
    return tuple(full)


def per_device(
    pixels,
    tile_slide,
    tile_count,
    w_patch,
    b_patch,
    dw_kernel,
    dw_bias,
    layernorm_gain,
    layernorm_bias,
    w_up,
    b_up,
    w_down,
    b_down,
    w_head,
    target,
):
    chan_count = lax.axis_size("chan")
    chan = lax.axis_index("chan")
    tile = lax.axis_index("tx") * lax.axis_size("tz") + lax.axis_index("tz")
    slot_count = tile_slide.shape[0]
    slots = slot_count // chan_count
    area = SIDE * SIDE
    slide_dev = target.shape[0]
    group_slides = slide_dev * lax.axis_size("tx") * lax.axis_size("tz")
    all_slides = group_slides * lax.axis_size("dp")

    shards = (
        w_patch,
        b_patch,
        dw_kernel,
        dw_bias,
        layernorm_gain,
        layernorm_bias,
        w_up,
        b_up,
        w_down,
        b_down,
        w_head,
    )
    full = gather_chan(shards, chan_count, spread=True)
    params = tuple(full[:10])
    head = full[10]

    my_pixels = lax.dynamic_slice_in_dim(pixels, chan * slots * area, slots * area, axis=1)
    my_slide = lax.dynamic_slice_in_dim(tile_slide, chan * slots, slots)
    slot_index = chan * slots + jnp.arange(slots, dtype=jnp.int32)
    live = (slot_index < tile_count[0]).astype(jnp.float32)
    onehot = (my_slide[:, None] == jnp.arange(group_slides, dtype=jnp.int32)[None, :]).astype(
        jnp.float32
    ) * live[:, None]

    pooled, pull = jax.vjp(lambda p: block_pooled(p, my_pixels), params)
    target_rows = jnp.zeros((slots,), jnp.float32)
    target_rows = lax.dynamic_update_slice_in_dim(target_rows, target, 0, axis=0)
    rows = jnp.concatenate(
        [
            pooled.T,
            my_slide.astype(jnp.float32)[:, None],
            live[:, None],
            jnp.where(chan == 0, target_rows, 0.0)[:, None],
        ],
        axis=1,
    )
    rows = gather_rows(rows, ("chan", "tx", "tz"))
    width = pooled.shape[0]
    onehot_all = (
        rows[:, width : width + 1] == jnp.arange(group_slides, dtype=jnp.float32)[None, :]
    ).astype(jnp.float32) * rows[:, width + 1 : width + 2]
    sums = jnp.dot(onehot_all.T, rows[:, :width], precision=highest)
    counts = jnp.maximum(jnp.sum(onehot_all, axis=0), 1.0)
    tile_of = np.arange(group_slides) // slide_dev
    where = tile_of * slots + np.arange(group_slides) % slide_dev
    target_all = rows[where, width + 2]

    slide_feat = sums / counts[:, None]
    logit = jnp.dot(slide_feat, head, precision=highest)
    error = logit - target_all
    loss_part = 0.5 * jnp.sum(error * error) / all_slides
    d_logit = error / all_slides
    g_head = jnp.dot(slide_feat.T, d_logit, precision=highest)
    d_sums = d_logit[:, None] * head[None, :] / counts[:, None]
    d_pooled = jnp.dot(onehot, d_sums, precision=highest).T
    grads = pull(d_pooled)[0]

    lead = tile == 0
    g_head = jnp.where(lead & (chan == 0), g_head, 0.0)
    flat = jnp.concatenate(
        [g.reshape(chan_count, -1) for g in grads] + [g_head.reshape(chan_count, -1)], axis=1
    )
    dp_count = lax.psum(1, "dp")
    flat = jnp.concatenate(
        [flat, jnp.where(lead & (chan == 0), loss_part, 0.0) * jnp.ones((chan_count, 1))], axis=1
    )
    length = flat.shape[1]
    x_count = lax.psum(1, "tx")
    pieces = dp_count * x_count
    half = -(-length // pieces)
    flat = jnp.pad(flat, ((0, 0), (0, half * pieces - length)))
    flat = flat.reshape(chan_count, dp_count, x_count, half).transpose(1, 0, 2, 3)
    mine = scatter_sum(flat.reshape(-1, half), ("dp", "chan", "tx"))
    mine = psum_steps(mine, ("tz",))
    mine = gather_rows(mine[None], ("dp", "tx")).reshape(-1)[:length]

    outs = []
    offset = 0
    for s in shards[:10] + shards[10:]:
        n = s.size
        outs.append(mine[offset : offset + n].reshape(s.shape))
        offset += n
    outs.append(mine[offset])
    return tuple(outs)


def solution(mesh):
    devices = np.asarray(mesh.devices)
    dp, tiles, chan = devices.shape
    grid = Mesh(devices.reshape(dp, X_SPAN, tiles // X_SPAN, chan), ("dp", "tx", "tz", "chan"))
    rows = ("dp", "tx", "tz")
    in_specs = (
        P(None, rows),
        P(rows),
        P(rows),
        P("chan", None),
        P("chan"),
        P("chan", None),
        P("chan"),
        P("chan"),
        P("chan"),
        P("chan", None),
        P("chan"),
        P("chan", None),
        P("chan"),
        P("chan"),
        P(rows),
    )
    out_specs = (
        P("chan", None),
        P("chan"),
        P("chan", None),
        P("chan"),
        P("chan"),
        P("chan"),
        P("chan", None),
        P("chan"),
        P("chan", None),
        P("chan"),
        P("chan"),
        P(),
    )
    return jax.shard_map(
        per_device, mesh=grid, in_specs=in_specs, out_specs=out_specs, check_vma=False
    )
```

```python
import jax
import jax.numpy as jnp
import numpy as np
from jax import lax
from jax.sharding import Mesh
from jax.sharding import PartitionSpec as P

SIDE = 8
X_SPAN = 4


epsilon = 1e-06
highest = lax.Precision.HIGHEST


def depthwise(stem_grid, kernel, bias):
    side_len = stem_grid.shape[-1]
    padded = jnp.pad(stem_grid, ((0, 0), (0, 0), (3, 3), (3, 3)))
    total = jnp.zeros_like(stem_grid)
    for kernel_row in range(7):
        for kernel_col in range(7):
            weight_tap = kernel[:, kernel_row * 7 + kernel_col][:, None, None, None]
            total = (
                total
                + weight_tap
                * padded[
                    :, :, kernel_row : kernel_row + side_len, kernel_col : kernel_col + side_len
                ]
            )
    return total + bias[:, None, None, None]


def block_pooled(params, pixels):
    w_patch, b_patch, dw_kernel, dw_bias, gain, shift, w_up, b_up, w_down, b_down = params
    width = w_patch.shape[0]
    tile_num = pixels.shape[1] // (SIDE * SIDE)
    stem = jnp.dot(w_patch, pixels, precision=highest) + b_patch[:, None]
    mixed = depthwise(stem.reshape(width, tile_num, SIDE, SIDE), dw_kernel, dw_bias).reshape(
        width, -1
    )
    average_value = jnp.mean(mixed, axis=0)
    variance = jnp.mean(mixed * mixed, axis=0) - average_value * average_value
    normed = (mixed - average_value) * lax.rsqrt(variance + epsilon) * gain[:, None] + shift[
        :, None
    ]
    pre_act = jnp.dot(w_up, normed, precision=highest) + b_up[:, None]
    hidden = jax.nn.gelu(pre_act, approximate=False)
    features = stem + jnp.dot(w_down.T, hidden, precision=highest) + b_down[:, None]
    return jnp.mean(features.reshape(width, tile_num, SIDE * SIDE), axis=2)


def spread_sum(value, axis):
    count = lax.psum(1, axis)
    copies = jnp.broadcast_to(value[None], (count,) + value.shape)
    return jnp.sum(lax.all_to_all(copies, axis, 0, 0, tiled=True), axis=0)


def gather_rows(value, axis):
    count = lax.psum(1, axis)
    copies = jnp.broadcast_to(value[None], (count,) + value.shape)
    return lax.all_to_all(copies, axis, 0, 0, tiled=True).reshape((-1,) + value.shape[1:])


def psum_steps(value, axes):
    for axis in axes:
        value = spread_sum(value, axis)
    return value


def scatter_sum(value, axis):
    return jnp.sum(lax.all_to_all(value, axis, 0, 0, tiled=True), axis=0)


def gather_chan(shards, chan_count, spread):
    packed = jnp.concatenate([s.reshape(1, -1) for s in shards], axis=1)
    if spread:
        copies = jnp.broadcast_to(packed, (chan_count, packed.shape[1]))
        gathered = lax.all_to_all(copies, "chan", 0, 0, tiled=True)
    else:
        gathered = lax.all_gather(packed, "chan", axis=0, tiled=True)
    full = []
    offset = 0
    for s in shards:
        n = s.size
        full.append(
            gathered[:, offset : offset + n].reshape((chan_count * s.shape[0],) + s.shape[1:])
        )
        offset += n
    return tuple(full)


def per_device(
    pixels,
    tile_slide,
    tile_count,
    w_patch,
    b_patch,
    dw_kernel,
    dw_bias,
    layernorm_gain,
    layernorm_bias,
    w_up,
    b_up,
    w_down,
    b_down,
    w_head,
    target,
):
    chan_count = lax.axis_size("chan")
    chan = lax.axis_index("chan")
    tile = lax.axis_index("tx") * lax.axis_size("tz") + lax.axis_index("tz")
    slot_count = tile_slide.shape[0]
    slots = slot_count // chan_count
    area = SIDE * SIDE
    slide_dev = target.shape[0]
    group_slides = slide_dev * lax.axis_size("tx") * lax.axis_size("tz")
    all_slides = group_slides * lax.axis_size("dp")

    shards = (
        w_patch,
        b_patch,
        dw_kernel,
        dw_bias,
        layernorm_gain,
        layernorm_bias,
        w_up,
        b_up,
        w_down,
        b_down,
        w_head,
    )
    full = gather_chan(shards, chan_count, spread=True)
    params = tuple(full[:10])
    head = full[10]

    my_pixels = lax.dynamic_slice_in_dim(pixels, chan * slots * area, slots * area, axis=1)
    my_slide = lax.dynamic_slice_in_dim(tile_slide, chan * slots, slots)
    slot_index = chan * slots + jnp.arange(slots, dtype=jnp.int32)
    live = (slot_index < tile_count[0]).astype(jnp.float32)
    onehot = (my_slide[:, None] == jnp.arange(group_slides, dtype=jnp.int32)[None, :]).astype(
        jnp.float32
    ) * live[:, None]

    pooled, pull = jax.vjp(lambda p: block_pooled(p, my_pixels), params)
    target_rows = jnp.zeros((slots,), jnp.float32)
    target_rows = lax.dynamic_update_slice_in_dim(target_rows, target, 0, axis=0)
    rows = jnp.concatenate(
        [
            pooled.T,
            my_slide.astype(jnp.float32)[:, None],
            live[:, None],
            jnp.where(chan == 0, target_rows, 0.0)[:, None],
        ],
        axis=1,
    )
    rows = gather_rows(rows, ("chan", "tx", "tz"))
    width = pooled.shape[0]
    onehot_all = (
        rows[:, width : width + 1] == jnp.arange(group_slides, dtype=jnp.float32)[None, :]
    ).astype(jnp.float32) * rows[:, width + 1 : width + 2]
    sums = jnp.dot(onehot_all.T, rows[:, :width], precision=highest)
    counts = jnp.maximum(jnp.sum(onehot_all, axis=0), 1.0)
    tile_of = np.arange(group_slides) // slide_dev
    where = tile_of * slots + np.arange(group_slides) % slide_dev
    target_all = rows[where, width + 2]

    slide_feat = sums / counts[:, None]
    logit = jnp.dot(slide_feat, head, precision=highest)
    error = logit - target_all
    loss_part = 0.5 * jnp.sum(error * error) / all_slides
    d_logit = error / all_slides
    g_head = jnp.dot(slide_feat.T, d_logit, precision=highest)
    d_sums = d_logit[:, None] * head[None, :] / counts[:, None]
    d_pooled = jnp.dot(onehot, d_sums, precision=highest).T
    grads = pull(d_pooled)[0]

    lead = tile == 0
    g_head = jnp.where(lead & (chan == 0), g_head, 0.0)
    flat = jnp.concatenate(
        [g.reshape(chan_count, -1) for g in grads] + [g_head.reshape(chan_count, -1)], axis=1
    )
    dp_count = lax.psum(1, "dp")
    flat = jnp.concatenate(
        [flat, jnp.where(lead & (chan == 0), loss_part, 0.0) * jnp.ones((chan_count, 1))], axis=1
    )
    length = flat.shape[1]
    x_count = lax.psum(1, "tx")
    z_count = lax.psum(1, "tz")
    pieces = dp_count * x_count * z_count
    half = -(-length // pieces)
    flat = jnp.pad(flat, ((0, 0), (0, half * pieces - length)))
    flat = flat.reshape(chan_count, dp_count, x_count, z_count, half).transpose(1, 0, 2, 3, 4)
    mine = scatter_sum(flat.reshape(-1, half), ("dp", "chan", "tx", "tz"))
    mine = gather_rows(mine[None], ("dp", "tx", "tz")).reshape(-1)[:length]

    outs = []
    offset = 0
    for s in shards[:10] + shards[10:]:
        n = s.size
        outs.append(mine[offset : offset + n].reshape(s.shape))
        offset += n
    outs.append(mine[offset])
    return tuple(outs)


def solution(mesh):
    devices = np.asarray(mesh.devices)
    dp, tiles, chan = devices.shape
    grid = Mesh(devices.reshape(dp, X_SPAN, tiles // X_SPAN, chan), ("dp", "tx", "tz", "chan"))
    rows = ("dp", "tx", "tz")
    in_specs = (
        P(None, rows),
        P(rows),
        P(rows),
        P("chan", None),
        P("chan"),
        P("chan", None),
        P("chan"),
        P("chan"),
        P("chan"),
        P("chan", None),
        P("chan"),
        P("chan", None),
        P("chan"),
        P("chan"),
        P(rows),
    )
    out_specs = (
        P("chan", None),
        P("chan"),
        P("chan", None),
        P("chan"),
        P("chan"),
        P("chan"),
        P("chan", None),
        P("chan"),
        P("chan", None),
        P("chan"),
        P("chan"),
        P(),
    )
    return jax.shard_map(
        per_device, mesh=grid, in_specs=in_specs, out_specs=out_specs, check_vma=False
    )
```
